32 devices in a mesh: dp: 8 (over z, y), tensor: 4 (over x, core).
Axes of the slice: x: 2, y: 2, z: 4, core: 2. Of those that a mesh axis runs over, the one named last changes fastest.
Arguments:
- hidden: bfloat16 [4096, 2048], P('dp'), may hold values from -6 to 6
- embedding: bfloat16 [4096, 2048], P('dp'), may hold values from -6 to 6
- teacher_mid: bfloat16 [4096, 2048], P('dp'), may hold values from -6 to 6
- teacher_out: bfloat16 [4096, 2048], P('dp'), may hold values from -6 to 6
- segment_ids: int32 [4096], P('dp'), may hold values from 0 to 7, as said below
- rope_pos: int32 [4096], P('dp'), may hold values from 0 to 255, as said below
- valid_mask: int32 [4096], P('dp'), may hold values from 0 to 1, as said below
- gain_attn: bfloat16 [4096], P('dp'), may hold values from 0.5 to 1.5
- w_query: bfloat16 [4096, 4096], P('dp', 'tensor'), may hold values from -0.09375 to 0.09375
- w_key: bfloat16 [4096, 4096], P('dp', 'tensor'), may hold values from -0.09375 to 0.09375
- w_value: bfloat16 [4096, 4096], P('dp', 'tensor'), may hold values from -0.09375 to 0.09375
- query_down: bfloat16 [4096, 128], P('dp'), may hold values from -0.09375 to 0.09375
- query_up: bfloat16 [128, 4096], P('dp', 'tensor'), may hold values from -0.25 to 0.25
- w_attn_out: bfloat16 [2048, 4096], P('dp', 'tensor'), may hold values from -0.75 to 0.75
- gain_mlp: bfloat16 [2048], P('dp'), may hold values from 0.5 to 1.5
- w_gate: bfloat16 [2048, 8192], P('dp', 'tensor'), may hold values from -0.125 to 0.125
- w_up: bfloat16 [2048, 8192], P('dp', 'tensor'), may hold values from -0.125 to 0.125
- gate_down: bfloat16 [2048, 128], P('dp'), may hold values from -0.125 to 0.125
- gate_up: bfloat16 [128, 8192], P('dp', 'tensor'), may hold values from -0.25 to 0.25
- w_down: bfloat16 [2048, 8192], P('dp', 'tensor'), may hold values from -0.0625 to 0.0625
- w_proj: bfloat16 [2048, 2048], P('dp', 'tensor'), may hold values from -0.125 to 0.125
- gain_mamba: bfloat16 [2048], P('dp'), may hold values from 0.5 to 1.5
- w_in_gate: bfloat16 [2048, 4096], P('dp', 'tensor'), may hold values from -0.125 to 0.125
- w_in_main: bfloat16 [2048, 4096], P('dp', 'tensor'), may hold values from -0.125 to 0.125
- w_in_state: bfloat16 [2048, 256], P('dp'), may hold values from -0.125 to 0.125
- w_in_step: bfloat16 [2048, 64], P('dp', 'tensor'), may hold values from -0.125 to 0.125
- conv_main: bfloat16 [4096, 4], P(('tensor', 'dp')), may hold values from -3 to 3
- conv_main_bias: bfloat16 [4096], P(('tensor', 'dp')), may hold values from -0.5 to 0.5
- conv_state: bfloat16 [256, 4], P('dp'), may hold values from -3 to 3
- conv_state_bias: bfloat16 [256], P('dp'), may hold values from -0.5 to 0.5
- gain_gated: bfloat16 [4096], P(('tensor', 'dp')), may hold values from 0.5 to 1.5
- w_mamba_out: bfloat16 [2048, 4096], P('dp', 'tensor'), may hold values from -0.09375 to 0.09375
- step_bias: bfloat16 [64], P('tensor'), may hold values from -5 to -2
- decay_log: bfloat16 [64], P('tensor'), may hold values from -1 to 2.5
- skip_scale: bfloat16 [64], P('tensor'), may hold values from 0.5 to 1.5
Outputs:
- output: bfloat16 [4096, 2048], P('dp')
- loss_mid: float32 [], replicated
- loss_out: float32 [], replicated
- grad_hidden: float32 [4096, 2048], P('dp')
- grad_embedding: float32 [4096, 2048], P('dp')
- grad_gain_attn: float32 [4096], P('dp')
- grad_w_query: float32 [4096, 4096], P('dp', 'tensor')
- grad_w_key: float32 [4096, 4096], P('dp', 'tensor')
- grad_w_value: float32 [4096, 4096], P('dp', 'tensor')
- grad_query_down: float32 [4096, 128], P('dp')
- grad_query_up: float32 [128, 4096], P('dp', 'tensor')
- grad_w_attn_out: float32 [2048, 4096], P('dp', 'tensor')
- grad_gain_mlp: float32 [2048], P('dp')
- grad_w_gate: float32 [2048, 8192], P('dp', 'tensor')
- grad_w_up: float32 [2048, 8192], P('dp', 'tensor')
- grad_gate_down: float32 [2048, 128], P('dp')
- grad_gate_up: float32 [128, 8192], P('dp', 'tensor')
- grad_w_down: float32 [2048, 8192], P('dp', 'tensor')
- grad_w_proj: float32 [2048, 2048], P('dp', 'tensor')
- grad_gain_mamba: float32 [2048], P('dp')
- grad_w_in_gate: float32 [2048, 4096], P('dp', 'tensor')
- grad_w_in_main: float32 [2048, 4096], P('dp', 'tensor')
- grad_w_in_state: float32 [2048, 256], P('dp')
- grad_w_in_step: float32 [2048, 64], P('dp', 'tensor')
- grad_conv_main: float32 [4096, 4], P(('tensor', 'dp'))
- grad_conv_main_bias: float32 [4096], P(('tensor', 'dp'))
- grad_conv_state: float32 [256, 4], P('dp')
- grad_conv_state_bias: float32 [256], P('dp')
- grad_gain_gated: float32 [4096], P(('tensor', 'dp'))
- grad_w_mamba_out: float32 [2048, 4096], P('dp', 'tensor')
- grad_step_bias: float32 [64], P('tensor')
- grad_decay_log: float32 [64], P('tensor')
- grad_skip_scale: float32 [64], P('tensor')
The draws below stay inside these ranges and needn't reach their ends.
Inputs may be any that keep to these rules, and one draw needn't show every extreme that they name: `segment_ids`: numbers count the documents of each sequence of 512 tokens from 0 and never fall inside it. `rope_pos`: the token's place within its document, 0 at a document's first token. `valid_mask`: the first token of every sequence is valid.
All inputs are finite; a program needn't handle non-finite values.
Results may differ from the reference program's by a relative error of at most 0.035.
Values may be sent and summed in bfloat16 or wider, within the bound.
No kernel may reach another device: no remote copies, remote signals or barrier semaphores. Data moves between devices by JAX's collectives and lax.ppermute only.
A program may use at most 384 MiB of HBM per device.

```python
from functools import partial
import jax
import jax.numpy as jnp
from jax import lax

D = 2048
HEADS = 32
HEAD_SIZE = 128
FF = 8192
RANK = 128
STATE = 128
NHM = 64
KW = 4
SEQ = 512
CAT = 4096
ATT = 4096
DI = 4096
HEAD_M = 64
TOKENS = 4096


def document_marks(key):
    rows = TOKENS // SEQ
    shortest = max(SEQ // 8, 1)
    longest = max(SEQ // 2, shortest + 1)
    pieces = SEQ // shortest + 1
    lengths = jax.random.randint(jax.random.fold_in(key, 11), (rows, pieces), shortest, longest + 1)
    lengths = lengths.at[rows - 1].set(shortest)
    lengths = lengths.at[0, 0].set(longest)
    ending = jnp.cumsum(lengths, axis=1)
    places = jnp.arange(SEQ, dtype=jnp.int32)
    passed = ending[:, None, :] <= places[None, :, None]
    segment = jnp.sum(passed.astype(jnp.int32), axis=2)
    starting = jnp.max(jnp.where(passed, ending[:, None, :], 0), axis=2)
    return (segment.astype(jnp.int32), (places[None, :] - starting).astype(jnp.int32))


def draw_segment_ids(key, part):
    return document_marks(key)[0].reshape(TOKENS)


def draw_rope_pos(key, part):
    return document_marks(key)[1].reshape(TOKENS)


def draw_valid_mask(key, part):
    rows = TOKENS // SEQ
    share = 30 + 60 * jnp.arange(rows, dtype=jnp.int32) // max(rows - 1, 1)
    rolled = jax.random.randint(jax.random.fold_in(key, 23), (rows, SEQ), 0, 100)
    valid = (rolled < share[:, None]).astype(jnp.int32)
    places = jnp.arange(SEQ, dtype=jnp.int32)
    valid = jnp.where(places[None, :] == 0, 1, valid)
    return valid.reshape(TOKENS).astype(jnp.int32)


def shard_levels(key, shape, shards, smallest, top_value):
    level, own = 1.0, jax.random.fold_in(key, 6)
    for position, parts in shards:
        heights = jnp.exp(jax.random.uniform(jax.random.fold_in(own, position), (parts,), jnp.float32, smallest / len(shards), top_value / len(shards)))
        level = level * jnp.repeat(heights, shape[position] // parts).reshape([-1 if axis == position else 1 for axis in range(len(shape))])
    return level


def noise(rng, extent, width, reach, shards=(), kind=jnp.bfloat16):
    drawn = width * jax.random.normal(rng, extent, jnp.float32)
    if shards:
        drawn = drawn * shard_levels(rng, extent, shards, -0.22, 0.18)
    return jnp.clip(drawn, -reach, reach).astype(kind)


def setup_inputs(seed: int = 0) -> dict:
    key_of = jax.random.split(jax.random.key(seed), 36)
    return {
        "hidden": noise(key_of[0], (TOKENS, D), 1.0, 6.0, ((0, 8),)),
        "embedding": noise(key_of[1], (TOKENS, D), 1.0, 6.0, ((0, 8),)),
        "teacher_mid": noise(key_of[2], (TOKENS, D), 1.0, 6.0, ((0, 8),)),
        "teacher_out": noise(key_of[3], (TOKENS, D), 1.0, 6.0, ((0, 8),)),
        "segment_ids": draw_segment_ids(jax.random.fold_in(key_of[35], 71), 0),
        "rope_pos": draw_rope_pos(jax.random.fold_in(key_of[35], 71), 0),
        "valid_mask": draw_valid_mask(jax.random.fold_in(key_of[35], 71), 0),
        "gain_attn": jnp.clip(1.0 + 0.1 * jax.random.normal(key_of[7], (CAT,), jnp.float32), 0.5, 1.5).astype(jnp.bfloat16),
        "w_query": noise(key_of[8], (CAT, ATT), CAT ** -0.5, 0.09375, ((0, 8), (1, 4))),
        "w_key": noise(key_of[9], (CAT, ATT), CAT ** -0.5, 0.09375, ((0, 8), (1, 4))),
        "w_value": noise(key_of[10], (CAT, ATT), CAT ** -0.5, 0.09375, ((0, 8), (1, 4))),
        "query_down": noise(key_of[11], (CAT, RANK), CAT ** -0.5, 0.09375, ((0, 8),)),
        "query_up": noise(key_of[12], (RANK, ATT), (4 * RANK) ** -0.5, 0.25, ((0, 8), (1, 4))),
        "w_attn_out": noise(key_of[13], (D, ATT), 64 ** -0.5, 0.75, ((0, 8), (1, 4))),
        "gain_mlp": jnp.clip(1.0 + 0.1 * jax.random.normal(key_of[14], (D,), jnp.float32), 0.5, 1.5).astype(jnp.bfloat16),
        "w_gate": noise(key_of[15], (D, FF), D ** -0.5, 0.125, ((0, 8), (1, 4))),
        "w_up": noise(key_of[16], (D, FF), D ** -0.5, 0.125, ((0, 8), (1, 4))),
        "gate_down": noise(key_of[17], (D, RANK), D ** -0.5, 0.125, ((0, 8),)),
        "gate_up": noise(key_of[18], (RANK, FF), (4 * RANK) ** -0.5, 0.25, ((0, 8), (1, 4))),
        "w_down": noise(key_of[19], (D, FF), FF ** -0.5, 0.0625, ((0, 8), (1, 4))),
        "w_proj": noise(key_of[20], (D, D), D ** -0.5, 0.125, ((0, 8), (1, 4))),
        "gain_mamba": jnp.clip(1.0 + 0.1 * jax.random.normal(key_of[21], (D,), jnp.float32), 0.5, 1.5).astype(jnp.bfloat16),
        "w_in_gate": noise(key_of[22], (D, DI), D ** -0.5, 0.125, ((0, 8), (1, 4))),
        "w_in_main": noise(key_of[23], (D, DI), D ** -0.5, 0.125, ((0, 8), (1, 4))),
        "w_in_state": noise(key_of[24], (D, 2 * STATE), D ** -0.5, 0.125, ((0, 8),)),
        "w_in_step": noise(key_of[25], (D, NHM), D ** -0.5, 0.125, ((0, 8), (1, 4))),
        "conv_main": noise(key_of[26], (DI, KW), KW ** -0.5, 3.0, ((0, 32),)),
        "conv_main_bias": jnp.clip(jax.random.uniform(key_of[27], (DI,), jnp.float32, -0.5, 0.5) * shard_levels(key_of[27], (DI,), ((0, 32),), -0.4, 0.0), -0.5, 0.5).astype(jnp.bfloat16),
        "conv_state": noise(key_of[28], (2 * STATE, KW), KW ** -0.5, 3.0, ((0, 8),)),
        "conv_state_bias": jnp.clip(jax.random.uniform(key_of[29], (2 * STATE,), jnp.float32, -0.5, 0.5) * shard_levels(key_of[29], (2 * STATE,), ((0, 8),), -0.4, 0.0), -0.5, 0.5).astype(jnp.bfloat16),
        "gain_gated": jnp.clip(1.0 + 0.1 * jax.random.normal(key_of[30], (DI,), jnp.float32), 0.5, 1.5).astype(jnp.bfloat16),
        "w_mamba_out": noise(key_of[31], (D, DI), DI ** -0.5, 0.09375, ((0, 8), (1, 4))),
        "step_bias": jnp.clip(-5.0 + 3.0 * jax.random.uniform(key_of[32], (NHM,), jnp.float32) ** shard_levels(key_of[32], (NHM,), ((0, 4),), -0.2, 0.2), -5.0, -2.0).astype(jnp.bfloat16),
        "decay_log": jnp.clip(-1.0 + 3.5 * jax.random.uniform(key_of[33], (NHM,), jnp.float32) ** shard_levels(key_of[33], (NHM,), ((0, 4),), -0.2, 0.2), -1.0, 2.5).astype(jnp.bfloat16),
        "skip_scale": jnp.clip(0.5 + 1.0 * jax.random.uniform(key_of[34], (NHM,), jnp.float32) ** shard_levels(key_of[34], (NHM,), ((0, 4),), -0.2, 0.2), 0.5, 1.5).astype(jnp.bfloat16),
    }


@jax.custom_vjp
def lower_precision(v):
    return lax.optimization_barrier(v.astype(jnp.bfloat16)).astype(jnp.float32)

@jax.custom_vjp
def lower_backward(v):
    return v

def low_keep(v):
    return (lower_precision(v), None)

def low_pass(kept, grad):
    return (grad,)

def back_keep(v):
    return (v, None)

def back_low(kept, grad):
    return (lower_precision(grad),)
lower_precision.defvjp(low_keep, low_pass)
lower_backward.defvjp(back_keep, back_low)
eps = 1e-05
highest_precision = lax.Precision.HIGHEST

def times_right(left, right):
    return jnp.dot(left, right, precision=highest_precision, preferred_element_type=jnp.float32)

def times_trans(left, right):
    return lax.dot_general(left, right, (((1,), (1,)), ((), ())), precision=highest_precision, preferred_element_type=jnp.float32)

def rms_scale(values, gain):
    return values * lax.rsqrt(lax.optimization_barrier(jnp.mean(values * values, axis=-1, keepdims=True)) + eps) * gain

def rotary(values, cosine, sine):
    half = values.shape[-1] // 2
    first = values[..., :half]
    second = values[..., half:]
    return jnp.concatenate([first * cosine - second * sine, second * cosine + first * sine], axis=-1)

def conv_act(pre, weight, bias, segments):
    length = pre.shape[1]
    total = jnp.zeros_like(pre) + bias
    for tap in range(KW):
        lag = KW - 1 - tap
        shifted = jnp.pad(pre, ((0, 0), (lag, 0), (0, 0)))[:, :length]
        earlier = jnp.pad(segments, ((0, 0), (lag, 0)), constant_values=-1)[:, :length]
        keeping = (earlier == segments).astype(jnp.float32)[:, :, None]
        total = total + weight[:, tap] * shifted * keeping
    return jax.nn.silu(total)

def attend_head(inputs, allowed):
    query_matrix_rows, key_matrix_rows, value_matrix_rows = inputs
    attention_scores = lower_backward(jnp.einsum('srw,sxw->srx', query_matrix_rows, key_matrix_rows, precision=highest_precision) * HEAD_SIZE ** (-0.5))
    attention_probabilities = jax.nn.softmax(jnp.where(allowed, attention_scores, -1e+30), axis=-1)
    return jnp.einsum('xnu,xuz->xnz', lower_precision(attention_probabilities), value_matrix_rows, precision=highest_precision)

def scan_head(inputs, gram, same):
    accum, weighted = inputs
    lagged = accum[:, :, None] - accum[:, None, :]
    kernel = jnp.where(same, jnp.exp(jnp.where(same, lagged, 0.0)), 0.0)
    mixing = lower_precision(gram * kernel)
    return jnp.einsum('bts,bse->bte', mixing, weighted, precision=highest_precision)

def layer(params, hidden, embedding, teacher_mid, teacher_out, segments, positions, valid, count):
    gain_attn, w_query, w_key, w_value, query_down, query_up, w_attn_out, gain_mlp, w_gate, w_up, gate_down, gate_up, w_down, w_proj, gain_mamba, w_in_gate, w_in_main, w_in_state, w_in_step, conv_main, conv_main_bias, conv_state, conv_state_bias, gain_gated, w_mamba_out, step_bias, decay_log, skip_scale = params
    batches = hidden.shape[0] // SEQ
    concat = jnp.concatenate([hidden, embedding], axis=1)
    normed_cat = lower_precision(rms_scale(concat, gain_attn))
    query_low = lower_precision(lower_backward(times_right(normed_cat, query_down)))
    query_pre = lower_backward(times_right(normed_cat, w_query) + times_right(query_low, query_up))
    key_pre = lower_backward(times_right(normed_cat, w_key))
    value_pre = lower_backward(times_right(normed_cat, w_value))
    half = HEAD_SIZE // 2
    inverse = 10000.0 ** (-jnp.arange(half, dtype=jnp.float32) / half)
    angles = positions.astype(jnp.float32)[:, None] * inverse[None, :]
    cosine = jnp.cos(angles)[:, None, :]
    sine = jnp.sin(angles)[:, None, :]
    query_rot = lower_precision(rotary(query_pre.reshape(-1, HEADS, HEAD_SIZE), cosine, sine))
    key_rot = lower_precision(rotary(key_pre.reshape(-1, HEADS, HEAD_SIZE), cosine, sine))
    value_low = lower_precision(value_pre)
    seg_rows = segments.reshape(batches, SEQ)
    places = jnp.arange(SEQ)
    causal = places[:, None] >= places[None, :]
    allowed = causal[None] & (seg_rows[:, :, None] == seg_rows[:, None, :])

    def heads_first(values, count_heads, size):
        return values.reshape(batches, SEQ, count_heads, size).transpose(2, 0, 1, 3)
    attended = lax.map(jax.checkpoint(partial(attend_head, allowed=allowed)), (heads_first(query_rot, HEADS, HEAD_SIZE), heads_first(key_rot, HEADS, HEAD_SIZE), heads_first(value_low, HEADS, HEAD_SIZE)))
    attended = attended.transpose(1, 2, 0, 3).reshape(-1, ATT)
    attended = lower_precision(lower_backward(attended))
    attn_branch = lower_backward(times_trans(attended, w_attn_out))
    first_sum = hidden + attn_branch
    normed_mid = lower_precision(rms_scale(first_sum, gain_mlp))
    gate_low = lower_precision(lower_backward(times_right(normed_mid, gate_down)))
    gate_pre = lower_backward(times_right(normed_mid, w_gate) + times_right(gate_low, gate_up))
    up_pre = lower_backward(times_right(normed_mid, w_up))
    inner = lower_precision(jax.nn.gelu(gate_pre, approximate=True) * up_pre)
    mlp_branch = lower_backward(times_trans(inner, w_down))
    shared_out = lower_precision(attn_branch + mlp_branch)
    projected = lower_backward(times_trans(shared_out, w_proj))
    middle = hidden + projected
    normed_last = lower_precision(rms_scale(middle, gain_mamba))
    mamba_gate = lower_backward(times_right(normed_last, w_in_gate))
    mamba_pre = lower_backward(times_right(normed_last, w_in_main))
    state_pre = lower_backward(times_right(normed_last, w_in_state))
    step_pre = lower_backward(times_right(normed_last, w_in_step))
    mamba_act = conv_act(mamba_pre.reshape(batches, SEQ, DI), conv_main, conv_main_bias, seg_rows)
    state_act = conv_act(state_pre.reshape(batches, SEQ, 2 * STATE), conv_state, conv_state_bias, seg_rows)
    state_in = lower_precision(state_act[..., :STATE])
    state_out = lower_precision(state_act[..., STATE:])
    step_sizes = jax.nn.softplus(step_pre.reshape(batches, SEQ, NHM) + step_bias)
    accum = jnp.cumsum(step_sizes * -jnp.exp(decay_log), axis=1)
    gram = lower_backward(jnp.einsum('bte,bse->bts', state_out, state_in, precision=highest_precision))
    mamba_heads = mamba_act.reshape(batches, SEQ, NHM, HEAD_M)
    weighted = lower_precision(mamba_heads * step_sizes[..., None])
    core = lax.map(jax.checkpoint(partial(scan_head, gram=gram, same=allowed)), (accum.transpose(2, 0, 1), weighted.transpose(2, 0, 1, 3)))
    core = lower_backward(core.transpose(1, 2, 0, 3))
    with_skip = (core + skip_scale[:, None] * mamba_heads).reshape(-1, DI)
    mixed = with_skip * jax.nn.silu(mamba_gate)
    normed_all = mixed * lax.rsqrt(lax.optimization_barrier(jnp.mean(mixed * mixed, axis=-1, keepdims=True)) + eps)
    gated_out = lower_precision(normed_all * gain_gated)
    mamba_branch = lower_backward(times_trans(gated_out, w_mamba_out))
    final_sum = middle + mamba_branch
    valid_rows = valid.astype(jnp.float32)[:, None]
    miss_mid = middle - teacher_mid
    miss_out = final_sum - teacher_out
    loss_mid = jnp.sum(valid_rows * miss_mid * miss_mid) / (count * D)
    loss_out = jnp.sum(valid_rows * miss_out * miss_out) / (count * D)
    objective = hidden.shape[0] * D / 2.0 * (loss_mid + loss_out)
    return (objective, (final_sum, loss_mid, loss_out))

def reference(hidden, embedding, teacher_mid, teacher_out, segment_ids, rope_pos, valid_mask, gain_attn, w_query, w_key, w_value, query_down, query_up, w_attn_out, gain_mlp, w_gate, w_up, gate_down, gate_up, w_down, w_proj, gain_mamba, w_in_gate, w_in_main, w_in_state, w_in_step, conv_main, conv_main_bias, conv_state, conv_state_bias, gain_gated, w_mamba_out, step_bias, decay_log, skip_scale):
    params = tuple((member.astype(jnp.float32) for member in (gain_attn, w_query, w_key, w_value, query_down, query_up, w_attn_out, gain_mlp, w_gate, w_up, gate_down, gate_up, w_down, w_proj, gain_mamba, w_in_gate, w_in_main, w_in_state, w_in_step, conv_main, conv_main_bias, conv_state, conv_state_bias, gain_gated, w_mamba_out, step_bias, decay_log, skip_scale)))
    count = jnp.sum(valid_mask.astype(jnp.float32))
    teacher_first = teacher_mid.astype(jnp.float32)
    teacher_last = teacher_out.astype(jnp.float32)

    def objective(weights, hidden_f, embed_f):
        return layer(weights, hidden_f, embed_f, teacher_first, teacher_last, segment_ids, rope_pos, valid_mask, count)
    total_value, back, extras = jax.vjp(objective, params, hidden.astype(jnp.float32), embedding.astype(jnp.float32), has_aux=True)
    weight_grads, grad_hidden, grad_embedding = back(jnp.ones((), jnp.float32))
    final_sum, loss_mid, loss_out = extras
    grad_gain_attn, grad_w_query, grad_w_key, grad_w_value, grad_query_down, grad_query_up, grad_w_attn_out, grad_gain_mlp, grad_w_gate, grad_w_up, grad_gate_down, grad_gate_up, grad_w_down, grad_w_proj, grad_gain_mamba, grad_w_in_gate, grad_w_in_main, grad_w_in_state, grad_w_in_step, grad_conv_main, grad_conv_main_bias, grad_conv_state, grad_conv_state_bias, grad_gain_gated, grad_w_mamba_out, grad_step_bias, grad_decay_log, grad_skip_scale = weight_grads
    return (final_sum.astype(jnp.bfloat16), loss_mid, loss_out, grad_hidden, grad_embedding, grad_gain_attn, grad_w_query, grad_w_key, grad_w_value, grad_query_down, grad_query_up, grad_w_attn_out, grad_gain_mlp, grad_w_gate, grad_w_up, grad_gate_down, grad_gate_up, grad_w_down, grad_w_proj, grad_gain_mamba, grad_w_in_gate, grad_w_in_main, grad_w_in_state, grad_w_in_step, grad_conv_main, grad_conv_main_bias, grad_conv_state, grad_conv_state_bias, grad_gain_gated, grad_w_mamba_out, grad_step_bias, grad_decay_log, grad_skip_scale)
```

```python
from functools import partial

import jax
import jax.numpy as jnp
from jax import lax
from jax.experimental import pallas as pl
from jax.experimental.pallas import tpu as pltpu
from jax.sharding import PartitionSpec as P

D = 2048
HEAD_SIZE = 128
STATE = 128
DI = 4096
HEAD_M = 64
PAIR = 2

eps = 1e-05
f32 = jnp.float32


def narrow(values):
    return values.astype(jnp.bfloat16)


def times_right(left, right, out=f32):
    return jnp.dot(left, right, preferred_element_type=f32).astype(out)


def times_trans(left, right, out=f32):
    return lax.dot_general(
        left, right, (((1,), (1,)), ((), ())), preferred_element_type=f32
    ).astype(out)


def trans_times(left, right, out=f32):
    return lax.dot_general(
        left, right, (((0,), (0,)), ((), ())), preferred_element_type=f32
    ).astype(out)


def rms_scale(values, gain):
    return values * lax.rsqrt(jnp.mean(values * values, axis=-1, keepdims=True) + eps) * gain


def flip(values, axis, bit):
    count = lax.axis_size(axis)
    return lax.ppermute(values, axis, [(i, i ^ bit) for i in range(count)])


def pick(values, axis, index):
    return lax.dynamic_index_in_dim(values, index, axis, keepdims=False)


def move_kernel(loads, stores, n_in, n_out, at_ref, *refs):
    ins, outs = refs[:n_in], refs[n_in : n_in + n_out]
    rooms, came, left = refs[n_in + n_out : -2], refs[-2], refs[-1]
    arrivals = []
    for i, (row, rows) in enumerate(loads):
        source = ins[i]
        if row is not None:
            source = source.at[pl.ds(pl.multiple_of(at_ref[row], rows), rows)]
        arrivals.append(pltpu.make_async_copy(source, rooms[i], came.at[i]))
        arrivals[-1].start()
    waiting, seen = [], set()
    for k, (i, column, width, out, row, to) in enumerate(stores):
        if i not in seen:
            arrivals[i].wait()
            seen.add(i)
        source = rooms[i].at[:, column : column + width]
        rows = loads[i][1]
        target = outs[out]
        if row is not None:
            target = target.at[pl.ds(pl.multiple_of(at_ref[row], rows), rows)]
        if isinstance(to, tuple):
            target = target.at[:, pl.ds(pl.multiple_of(at_ref[to[0]], width), width)]
        else:
            target = target.at[:, to : to + width]
        waiting.append(pltpu.make_async_copy(source, target, left.at[k]))
        waiting[-1].start()
    for store in waiting:
        store.wait()


def move(pieces, at, loads, stores, shapes):
    dtype = pieces[0].dtype
    at = jnp.stack(at).astype(jnp.int32) if at else jnp.zeros((1,), jnp.int32)
    return pl.pallas_call(
        partial(move_kernel, tuple(loads), tuple(stores), len(pieces), len(shapes)),
        out_shape=[jax.ShapeDtypeStruct(shape, dtype) for shape in shapes],
        in_specs=[pl.BlockSpec(memory_space=pltpu.SMEM)]
        + [pl.BlockSpec(memory_space=pl.ANY)] * len(pieces),
        out_specs=[pl.BlockSpec(memory_space=pl.ANY)] * len(shapes),
        scratch_shapes=[
            pltpu.VMEM((load[1], piece.shape[1]), dtype) for load, piece in zip(loads, pieces)
        ]
        + [pltpu.SemaphoreType.DMA((len(pieces),)), pltpu.SemaphoreType.DMA((len(stores),))],
    )(at, *pieces)


def place(pieces, starts, along, total, columns=None, widths=None):
    shape = list(pieces[0].shape)
    wide = shape[1]
    shape[along] = total
    if widths is not None:
        stores = []
        for i in range(len(pieces)):
            first = 0
            for out, width in enumerate(widths):
                stores.append((i, first, width, out, i, 0))
                first += width
        loads = [(None, piece.shape[0]) for piece in pieces]
        return move(pieces, starts, loads, stores, [(total, width) for width in widths])
    columns = columns or [(0, wide, 0)]
    stores = []
    for i in range(len(pieces)):
        for first, width, to in columns:
            if along == 0:
                stores.append((i, first, width, 0, i, to))
            else:
                stores.append((i, 0, wide, 0, None, (i,)))
    loads = [(None, piece.shape[0]) for piece in pieces]
    return move(pieces, starts, loads, stores, [tuple(shape)])[0]


class Place:
    def __init__(self):
        self.dp = lax.axis_index("dp")
        self.tensor = lax.axis_index("tensor")
        self.n_dp = lax.axis_size("dp")
        self.z = (self.dp // PAIR) % 2
        self.x = self.tensor // 2
        self.c = self.tensor % 2
        bits = [1 << k for k in range(self.n_dp.bit_length() - 1)]
        self.dp_bits = bits
        self.far_bits = [b for b in bits if b not in (1, PAIR)]
        self.pairs = [[i, i + 1] for i in range(0, self.n_dp, 2)]
        self.square = [
            [y + PAIR * z + 4 * far for y in (0, 1) for far in range(self.n_dp // 4)]
            for z in (0, 1)
        ]
        self.gates = {"pair": [], "far": []}
        self.marks = {}

    def dp_bit(self, bit):
        return (self.dp // bit) % 2


    def half(self, shard, which):
        width = shard.shape[1] // 2
        return lax.dynamic_slice_in_dim(shard, which * width, width, 1)

    def send(self, values, bit):
        gate = self.gates["pair" if bit == PAIR else "far"]
        if gate:
            values = lax.optimization_barrier((values, *gate))[0]
        came = flip(values, "dp", bit)
        gate[:] = [came]
        return came

    def blocks(self, values, axis, order):
        size = values.shape[axis] // self.n_dp
        parts = [lax.slice_in_dim(values, i * size, (i + 1) * size, axis=axis) for i in order]
        return jnp.concatenate(parts, axis)

    def ordered(self, values, axis):
        order = [i for low in (0, 1) for i in range(low, self.n_dp, 2)]
        return self.blocks(values, axis, order)

    def restored(self, values, axis):
        half = self.n_dp // 2
        return self.blocks(values, axis, [i // 2 + half * (i % 2) for i in range(self.n_dp)])

    def columns_ordered(self, wide, first=0):
        size, half = wide // self.n_dp, self.n_dp // 2
        return [
            (first + i * size, size, (i % 2 * half + i // 2) * size) for i in range(self.n_dp)
        ]

    def columns_restored(self, wide):
        return [(to, size, first) for first, size, to in self.columns_ordered(wide)]

    def restored_rows(self, values):
        rows, wide = values.shape
        if wide // self.n_dp % 128:
            return self.restored(values, 1)
        stores = [(0, c, w, 0, None, to) for c, w, to in self.columns_restored(wide)]
        return move([values], [], [(None, rows)], stores, [values.shape])[0]

    def after(self, values, *names):
        return lax.optimization_barrier((values, *(self.marks[n] for n in names)))[0]

    def halves(self, shards, extra=()):
        mine = jnp.concatenate([*(self.half(s, self.z) for s in shards), *extra], 1)
        partner = jnp.concatenate([*(self.half(s, 1 - self.z) for s in shards), *extra], 1)
        return mine, partner

    def near_gather(self, line):
        return lax.all_gather(line, "dp", axis=0, tiled=True, axis_index_groups=self.pairs)

    def swap(self, *shards, extra=()):
        mine, partner = self.halves(shards, extra)
        return mine, self.send(partner, PAIR)

    def gather_weight(self, mine, came, *early):
        pieces = {0: mine, PAIR: came}
        for bit in self.far_bits:
            for mask in list(pieces):
                pieces[mask | bit] = self.send(pieces[mask], bit)
        rows = mine.shape[0]
        starts = [((self.dp ^ mask) // 2) * rows for mask in pieces]
        line = place(list(pieces.values()), starts, 0, self.n_dp // 2 * rows)
        self.gates["far"] += [line, *early]
        return self.near_gather(line)

    def start_line(self, name, mine, came):
        rows = mine.shape[0]
        line = place([mine, came], [self.z * rows, (1 - self.z) * rows], 0, 2 * rows)
        self.marks[name + ".pair"] = line
        return line

    def finish_line(self, name, line, widths=None, hold=None):
        for bit in self.far_bits:
            rows = line.shape[0]
            came = self.send(line, bit)
            if hold is not None:
                came = lax.optimization_barrier((came, hold))[0]
            own = self.dp_bit(bit)
            cut = widths if bit == self.far_bits[-1] else None
            line = place([line, came], [own * rows, (1 - own) * rows], 0, 2 * rows, widths=cut)
        self.marks[name + ".far"] = came
        self.marks[name + ".line"] = line if widths is None else line[0]
        return line

    def gather_packed(self, packed):
        value = packed[None]
        for bit in [PAIR] + self.far_bits:
            other = flip(value, "dp", bit)
            low = self.dp_bit(bit) == 0
            value = jnp.concatenate(
                [jnp.where(low, value, other), jnp.where(low, other, value)]
            )
        other = flip(value, "dp", 1)
        value = jnp.where(
            self.dp % 2 == 0, jnp.stack([value, other], 1), jnp.stack([other, value], 1)
        )
        return value.reshape((-1,) + packed.shape)

    def split_dp(self, values):
        rows = values.shape[0] // self.n_dp
        return values.reshape((2,) * len(self.dp_bits) + (rows,) + values.shape[1:])

    def sum_dp(self, values):
        values = self.split_dp(values)
        for k, bit in enumerate(reversed(self.dp_bits)):
            mine = self.dp_bit(bit)
            away = narrow(pick(values, 0, 1 - mine))
            kept = pick(values, 0, mine).astype(f32)
            values = narrow(kept + flip(away, "dp", bit).astype(f32))
        return values

    def near_sum(self, grad):
        return lax.psum_scatter(
            grad, "dp", scatter_dimension=0, tiled=True, axis_index_groups=self.pairs
        )

    def square_sum(self, grad):
        return lax.psum_scatter(
            grad, "dp", scatter_dimension=0, tiled=True, axis_index_groups=self.square
        )

    def join_halves(self, name, *summed, parts=None):
        values = [v.reshape(2, v.shape[0] // 2, v.shape[1]) for v in summed]
        return self.join(name, values, parts)

    def scatter_unit(self, name, *summed, parts=None):
        rows = 2 * summed[0].shape[0] // self.n_dp
        left = [b for b in reversed(self.dp_bits) if b != 1]
        values = [v.reshape((2,) * len(left) + (rows, v.shape[1])) for v in summed]
        for bit in self.far_bits:
            at = left.index(bit)
            mine = self.dp_bit(bit)
            away = jnp.concatenate([pick(v, at, 1 - mine) for v in values], -1)
            if bit == self.far_bits[0]:
                self.marks[name + ".ready"] = away
            came = self.send(away, bit)
            first, added = 0, []
            for v in values:
                width = v.shape[-1]
                part = came[..., first : first + width].astype(f32)
                added.append(narrow(pick(v, at, mine).astype(f32) + part))
                first += width
            values = added
            left.pop(at)
        self.marks[name + ".sum"] = came
        return self.join(name, values, parts)

    def join(self, name, values, parts):
        away = jnp.concatenate([pick(v, 0, 1 - self.z) for v in values], -1)
        self.marks[name + ".turn"] = away
        other = self.send(away, PAIR)
        self.marks[name + ".swap"] = other
        out, first = [], 0
        for v, count in zip(values, parts or (1,) * len(values)):
            mine = pick(v, 0, self.z)
            width = v.shape[-1] // count
            for i in range(count):
                a = mine[:, i * width : (i + 1) * width]
                b = other[:, first : first + width]
                joined = jnp.where(
                    self.z == 0, jnp.concatenate([a, b], 1), jnp.concatenate([b, a], 1)
                )
                out.append(joined.astype(f32))
                first += width
        return out


    def hop(self, values, name):
        if name == "z":
            return flip(values, "dp", PAIR)
        return flip(values, "tensor", 2 if name == "x" else 1)

    def halve(self, values, order, names, kind=jnp.bfloat16):
        order = list(order)
        for name in names:
            at = order.index(name)
            mine = getattr(self, name)
            away = pick(values, at, 1 - mine).astype(kind)
            kept = pick(values, at, mine).astype(f32)
            values = kept + self.hop(away, name).astype(f32)
            order.pop(at)
            if order:
                values = values.astype(kind)
        return values

    def reduce_tokens(self, part):
        rows, wide = part.shape
        blocks = part.reshape(2, 2, 2, rows // 8, wide)
        first = self.halve(blocks, "zxc", "c")
        cut = wide // 2
        return jnp.concatenate(
            [
                self.halve(narrow(first)[..., :cut], "zx", "xz"),
                self.halve(narrow(first)[..., cut:], "zx", "zx"),
            ],
            -1,
        )

    def reduce_features(self, part):
        if self.n_dp != 8:
            wide, rows = part.shape
            part = self.restored(part, 0).reshape(2, 2, 2, wide // 8, rows)
            part = part.transpose(2, 0, 1, 3, 4).reshape(wide, rows)
        return self.reduce_tokens(part)

    def spread(self, shard, cut_at):
        by_z = self.hop(shard, "z")
        by_x = self.hop(shard, "x")
        far_a = self.hop(by_z[:cut_at], "x")
        far_b = self.hop(by_x[cut_at:], "z")
        pieces = [(0, 0, None, shard), (1, 0, None, by_z), (0, 1, None, by_x)]
        pieces += [(1, 1, 0, far_a), (1, 1, 1, far_b)]
        out = []
        for dz, dx, part, piece in pieces:
            out.append((dz, dx, 0, part, piece))
            out.append((dz, dx, 1, part, self.hop(piece, "c")))
        return out

    def gather_tokens(self, shard):
        rows = shard.shape[0]
        pieces, starts = [], []
        for dz, dx, dc, part, piece in self.spread(shard, rows // 2):
            block = (self.z ^ dz) * 4 + (self.x ^ dx) * 2 + (self.c ^ dc)
            starts.append(block * rows + (rows // 2 if part == 1 else 0))
            pieces.append(piece)
        return place(pieces, starts, 0, 8 * rows)

    def gather_features(self, shard):
        wide = shard.shape[1]
        by_z = self.hop(shard, "z")
        by_x = self.hop(shard, "x")
        far = self.hop(by_z, "x")
        pieces, starts = [], []
        for dz, dx, piece in ((0, 0, shard), (1, 0, by_z), (0, 1, by_x), (1, 1, far)):
            for dc, value in ((0, piece), (1, self.hop(piece, "c"))):
                block = (self.x ^ dx) * 4 + (self.c ^ dc) * 2 + (self.z ^ dz)
                if self.n_dp == 8:
                    block = block % 2 * 4 + block // 2
                starts.append(block * wide)
                pieces.append(value)
        whole = place(pieces, starts, 1, 8 * wide)
        return whole if self.n_dp == 8 else self.ordered(whole, 1)

    def gather_own(self, shard, columns=None):
        rows = shard.shape[0]
        by_x = self.hop(shard, "x")
        pieces, starts = [], []
        for dx, piece in ((0, shard), (1, by_x)):
            for dc, value in ((0, piece), (1, self.hop(piece, "c"))):
                starts.append(((self.x ^ dx) * 2 + (self.c ^ dc)) * rows)
                pieces.append(value)
        return place(pieces, starts, 0, 4 * rows, columns)

    def gather_small(self, row):
        value = row
        for name in "cxz":
            mine = getattr(self, name)
            other = self.hop(value, name)
            value = jnp.where(
                mine == 0,
                jnp.concatenate([value, other]),
                jnp.concatenate([other, value]),
            )
        return value

    def sum_everywhere(self, values, tensor=True):
        for bit in self.dp_bits:
            values = values + flip(values, "dp", bit)
        if tensor:
            for bit in (1, 2):
                values = values + flip(values, "tensor", bit)
        return values


def small_rows(size):
    return -(-size // 128)


def pack(arrays, lead):
    rows = []
    for a in arrays:
        flat = a.reshape(lead, -1)
        size = flat.shape[1]
        flat = jnp.pad(flat, ((0, 0), (0, small_rows(size) * 128 - size)))
        rows.append(flat.reshape(lead, -1, 128))
    total = sum(r.shape[1] for r in rows)
    fill = -total % 64
    if fill:
        rows.append(jnp.zeros((lead, fill, 128), arrays[0].dtype))
    return jnp.concatenate(rows, 1)


def unpack(packed, shapes):
    out, at = [], 0
    lead = packed.shape[0]
    for shape in shapes:
        size = 1
        for s in shape:
            size *= s
        rows = small_rows(size)
        part = packed[:, at : at + rows].reshape(lead, rows * 128)[:, :size]
        out.append(part.reshape((lead,) + tuple(shape)))
        at += rows
    return out


def rows_joined(values):
    return values.reshape((values.shape[0] * values.shape[1],) + values.shape[2:])


def conv_act(pre, weight, bias, segments):
    length = pre.shape[1]
    taps = weight.shape[1]
    total = jnp.zeros_like(pre) + bias
    for tap in range(taps):
        lag = taps - 1 - tap
        shifted = jnp.pad(pre, ((0, 0), (lag, 0), (0, 0)))[:, :length]
        earlier = jnp.pad(segments, ((0, 0), (lag, 0)), constant_values=-1)[:, :length]
        keeping = (earlier == segments).astype(f32)[:, :, None]
        total = total + weight[:, tap] * shifted * keeping
    return jax.nn.silu(total)


def gelu_product(gate_pre, up_pre):
    return jax.nn.gelu(gate_pre, approximate=True) * up_pre


def decay_piece(step_pre, step_bias, decay_log):
    sizes = jax.nn.softplus(step_pre + step_bias)
    return (jnp.cumsum(sizes * -jnp.exp(decay_log), axis=1), sizes)


def mixed_piece(core, mamba_act, mamba_gate, skip_scale):
    wide = jnp.broadcast_to(skip_scale[:, None], (skip_scale.shape[0], HEAD_M)).reshape(-1)
    with_skip = core + wide * mamba_act
    return with_skip * jax.nn.silu(mamba_gate)


def dot_nn(left, right):
    return jnp.dot(left, right, preferred_element_type=f32)


def dot_nt(left, right):
    return lax.dot_general(left, right, (((1,), (1,)), ((), ())), preferred_element_type=f32)


def dot_tn(left, right):
    return lax.dot_general(left, right, (((0,), (0,)), ((), ())), preferred_element_type=f32)


def same_document(down, across):
    shape = (down.shape[0], across.shape[1])
    later = lax.broadcasted_iota(jnp.int32, shape, 0) >= lax.broadcasted_iota(
        jnp.int32, shape, 1
    )
    return later & (down == across)


def turn(values, cosine, sine):
    return values * cosine + pltpu.roll(values, HEAD_SIZE // 2, 1) * sine


def attend_probabilities(query, key, kept):
    scores = jnp.where(kept, dot_nt(query, key) * HEAD_SIZE ** (-0.5), -1e30)
    raised = jnp.exp(scores - jnp.max(scores, axis=1, keepdims=True))
    return raised / jnp.sum(raised, axis=1, keepdims=True)


def attend_kernel(q_ref, k_ref, v_ref, cos_ref, sin_ref, down_ref, across_ref, qo, ko, out):
    cosine, sine = cos_ref[...], sin_ref[...]
    query = narrow(turn(q_ref[...], cosine, sine))
    key = narrow(turn(k_ref[...], cosine, sine))
    qo[...] = query
    ko[...] = key
    kept = same_document(down_ref[...], across_ref[...])
    probabilities = narrow(attend_probabilities(query, key, kept))
    out[...] = narrow(dot_nn(probabilities, v_ref[...]))


def attend_back_kernel(
    q_ref, k_ref, v_ref, g_ref, cos_ref, sin_ref, down_ref, across_ref, dq, dk, dv
):
    query, key, grad = q_ref[...], k_ref[...], g_ref[...]
    kept = same_document(down_ref[...], across_ref[...])
    probabilities = attend_probabilities(query, key, kept)
    dv[...] = narrow(dot_tn(narrow(probabilities), grad))
    grad_probs = dot_nt(grad, v_ref[...])
    inner = jnp.sum(probabilities * grad_probs, axis=1, keepdims=True)
    grad_scores = narrow(probabilities * (grad_probs - inner))
    cosine, sine = cos_ref[...], sin_ref[...]
    scale = HEAD_SIZE ** (-0.5)
    dq[...] = narrow(turn(dot_nn(grad_scores, key) * scale, cosine, -sine))
    dk[...] = narrow(turn(dot_tn(grad_scores, query) * scale, cosine, -sine))


def of_head(j):
    lane = lax.broadcasted_iota(jnp.int32, (1, 2 * HEAD_M), 1)
    return (lane >= j * HEAD_M) & (lane < (j + 1) * HEAD_M)


def decay_of(acc_ref, turned_ref, j, kept):
    lagged = acc_ref[:, j : j + 1] - turned_ref[j : j + 1, :]
    return jnp.where(kept, jnp.exp(jnp.where(kept, lagged, 0.0)), 0.0)


def weighted_of(act_ref, size_ref):
    return narrow(act_ref[...] * jnp.where(of_head(0), size_ref[:, 0:1], size_ref[:, 1:2]))


def mix_kernel(act_ref, size_ref, acc_ref, turned_ref, in_ref, out_ref, down_ref, across_ref, core):
    kept = same_document(down_ref[...], across_ref[...])
    gram = dot_nt(out_ref[...], in_ref[...])
    weighted = weighted_of(act_ref, size_ref)
    parts = [
        dot_nn(narrow(gram * decay_of(acc_ref, turned_ref, j, kept)), weighted) for j in (0, 1)
    ]
    core[...] = jnp.where(of_head(0), parts[0], parts[1])


def mix_back_kernel(
    grad_ref,
    act_ref,
    size_ref,
    acc_ref,
    turned_ref,
    in_ref,
    out_ref,
    down_ref,
    across_ref,
    dact,
    dsize,
    dgram,
    dacc,
    dturned,
    total,
):
    kept = same_document(down_ref[...], across_ref[...])
    gram = dot_nt(out_ref[...], in_ref[...])
    weighted = weighted_of(act_ref, size_ref)
    grad = grad_ref[...]

    @pl.when(pl.program_id(1) == 0)
    def _():
        total[...] = jnp.zeros_like(total)

    parts = []
    for j in (0, 1):
        decay = decay_of(acc_ref, turned_ref, j, kept)
        mixing = gram * decay
        parts.append(dot_tn(narrow(mixing), grad))
        grad_mixing = dot_nt(jnp.where(of_head(j), grad, jnp.zeros_like(grad)), weighted)
        total[...] += grad_mixing * decay
        grad_lag = grad_mixing * mixing
        dacc[:, j : j + 1] = jnp.sum(grad_lag, axis=1, keepdims=True)
        dturned[j : j + 1, :] = jnp.sum(grad_lag, axis=0, keepdims=True)
    grad_weighted = jnp.where(of_head(0), parts[0], parts[1])
    dact[...] = grad_weighted * jnp.where(of_head(0), size_ref[:, 0:1], size_ref[:, 1:2])
    product = grad_weighted * act_ref[...]
    for j in (0, 1):
        dsize[:, j : j + 1] = jnp.sum(
            jnp.where(of_head(j), product, 0.0), axis=1, keepdims=True
        )

    @pl.when(pl.program_id(1) == pl.num_programs(1) - 1)
    def _():
        dgram[...] = narrow(total[...])


def by_columns(S):
    return pl.BlockSpec((S, 128), lambda b, h: (b, h))


def by_sequence(S):
    return pl.BlockSpec((S, 128), lambda b, h: (b, 0))


def marks_specs(S):
    return [
        pl.BlockSpec((S, 1), lambda b, h: (b, 0)),
        pl.BlockSpec((None, 1, S), lambda b, h: (b, 0, 0)),
    ]


def attend_forward(query_pre, key_pre, value_low, cosine, sine, marks):
    T, wide = query_pre.shape
    S = T // 2
    low = jax.ShapeDtypeStruct((T, wide), jnp.bfloat16)
    return pl.pallas_call(
        attend_kernel,
        grid=(2, wide // 128),
        in_specs=[by_columns(S)] * 3 + [by_sequence(S)] * 2 + marks_specs(S),
        out_specs=[by_columns(S)] * 3,
        out_shape=[low] * 3,
    )(query_pre, key_pre, value_low, cosine, sine, *marks)


def attend_backward(query_rot, key_rot, value_low, grad, cosine, sine, marks):
    T, wide = query_rot.shape
    S = T // 2
    low = jax.ShapeDtypeStruct((T, wide), jnp.bfloat16)
    return pl.pallas_call(
        attend_back_kernel,
        grid=(2, wide // 128),
        in_specs=[by_columns(S)] * 4 + [by_sequence(S)] * 2 + marks_specs(S),
        out_specs=[by_columns(S)] * 3,
        out_shape=[low] * 3,
    )(query_rot, key_rot, value_low, grad, cosine, sine, *marks)


def by_heads(values):
    _, S, heads = values.shape
    turned = values.transpose(0, 2, 1).reshape(2, heads // 2, 2, S)
    return turned.transpose(0, 1, 3, 2), turned


def heads_specs(S):
    return (
        pl.BlockSpec((None, None, S, 2), lambda b, h: (b, h, 0, 0)),
        pl.BlockSpec((None, None, 2, S), lambda b, h: (b, h, 0, 0)),
    )


def mix_forward(act, sizes, accum, accum_turned, state_in, state_out, marks):
    T, wide = act.shape
    S = T // 2
    down, across = heads_specs(S)
    return pl.pallas_call(
        mix_kernel,
        grid=(2, wide // 128),
        in_specs=[by_columns(S), down, down, across]
        + [by_sequence(S)] * 2
        + marks_specs(S),
        out_specs=by_columns(S),
        out_shape=jax.ShapeDtypeStruct((T, wide), f32),
    )(act, sizes, accum, accum_turned, state_in, state_out, *marks)


def mix_backward(grad, act, sizes, accum, accum_turned, state_in, state_out, marks):
    T, wide = act.shape
    S = T // 2
    down, across = heads_specs(S)
    return pl.pallas_call(
        mix_back_kernel,
        grid=(2, wide // 128),
        in_specs=[by_columns(S), by_columns(S), down, down, across]
        + [by_sequence(S)] * 2
        + marks_specs(S),
        out_specs=[
            by_columns(S),
            down,
            pl.BlockSpec((None, S, S), lambda b, h: (b, 0, 0)),
            down,
            across,
        ],
        out_shape=[
            jax.ShapeDtypeStruct((T, wide), f32),
            jax.ShapeDtypeStruct(accum.shape, f32),
            jax.ShapeDtypeStruct((2, S, S), jnp.bfloat16),
            jax.ShapeDtypeStruct(accum.shape, f32),
            jax.ShapeDtypeStruct(accum_turned.shape, f32),
        ],
        scratch_shapes=[pltpu.VMEM((S, S), f32)],
    )(grad, act, sizes, accum, accum_turned, state_in, state_out, *marks)


def body(
    hidden,
    embedding,
    teacher_mid,
    teacher_out,
    segment_ids,
    rope_pos,
    valid_mask,
    gain_attn,
    w_query,
    w_key,
    w_value,
    query_down,
    query_up,
    w_attn_out,
    gain_mlp,
    w_gate,
    w_up,
    gate_down,
    gate_up,
    w_down,
    w_proj,
    gain_mamba,
    w_in_gate,
    w_in_main,
    w_in_state,
    w_in_step,
    conv_main,
    conv_main_bias,
    conv_state,
    conv_state_bias,
    gain_gated,
    w_mamba_out,
    step_bias,
    decay_log,
    skip_scale,
):
    me = Place()
    n_dp = me.n_dp
    S = hidden.shape[0]
    T = 2 * S
    quarter = S // 4
    z = me.z

    def own_rows(values):
        return lax.dynamic_slice_in_dim(values, me.tensor * quarter, quarter, 0)

    def own_tokens(values):
        return lax.dynamic_slice_in_dim(values, (z * 4 + me.tensor) * quarter, quarter, 0)

    def own_half(values, axis=-1):
        axis = axis % values.ndim
        width = values.shape[axis] // 2
        return lax.dynamic_slice_in_dim(values, z * width, width, axis)

    def filled(values, rows):
        fill = rows - values.shape[0]
        return jnp.pad(values, ((0, fill), (0, 128 - values.shape[1])))

    tiny = (
        gain_mlp,
        gain_mamba,
        conv_main,
        conv_main_bias,
        conv_state,
        conv_state_bias,
        gain_gated,
    )
    tiny_shapes = tuple(a.shape for a in tiny)
    tiny_pack = pack([a[None] for a in tiny], 1)[0]
    row_count = w_attn_out.shape[0]
    marks = jnp.stack([segment_ids, rope_pos])
    marks_other = me.hop(marks, "z")
    small = me.gather_packed(pack([gain_attn[None], query_up[None]], 1)[0])
    gain_attn_all, query_up_all = map(
        rows_joined, unpack(small, (gain_attn.shape, query_up.shape))
    )
    query_up_all = own_half(query_up_all)
    marks = jnp.stack([segment_ids, rope_pos])
    marks_other = me.hop(marks, "z")
    own_cat = jnp.concatenate([hidden, embedding], 1)
    gain_attn_f = gain_attn_all.astype(f32)
    normed_own = narrow(rms_scale(own_cat.astype(f32), gain_attn_f))
    normed_came = me.hop(own_rows(normed_own), "z")
    near_lane, far_lane = me.gates["pair"], me.gates["far"]
    swaps = {"query": me.swap(w_query)}
    near_lane += [small, marks_other]
    swaps["key"] = me.swap(w_key)
    near_lane += [normed_came]
    swaps["value"] = me.swap(w_value, extra=(query_down,))
    swaps["attn_out"] = me.swap(
        w_attn_out,
        extra=(
            gate_down,
            w_in_state,
            filled(gate_up.reshape(-1, 128), row_count),
            filled(w_in_step, row_count),
            filled(tiny_pack, row_count),
        ),
    )
    swaps["gate_up"] = me.swap(w_gate, w_up)
    swaps["late"] = me.swap(w_down, w_proj, w_in_gate, w_in_main, w_mamba_out)
    w_query_all = me.gather_weight(*swaps["query"])
    w_key_all = me.gather_weight(*swaps["key"])
    w_value_more = me.gather_weight(*swaps["value"])
    far_lane += [swaps["gate_up"][1]]
    attn_out_line = me.start_line("attn_out", *swaps["attn_out"])
    gate_up_line = me.start_line("gate_up", *swaps["gate_up"])
    late_line = me.start_line("late", *swaps["late"])
    w_attn_out_more = me.near_gather(me.finish_line("attn_out", attn_out_line))
    far_lane += [swaps["late"][1]]
    units = w_down.shape[1] // 2
    channels = w_in_gate.shape[1] // 2
    wide = w_value.shape[1] // 2
    w_value_all = w_value_more[:, :wide]
    query_down_all = w_value_more[:, wide:]

    def rows_back(columns, like):
        flat = columns.reshape(n_dp, -1, 128)[:, : like.size // 128]
        return rows_joined(me.restored(flat, 0).reshape((n_dp,) + like.shape))

    wide = w_attn_out.shape[1] // 2
    w_attn_out_all = w_attn_out_more[:, :wide]
    more = w_attn_out_more[:, wide:]
    gate_down_all = more[:, :128]
    w_in_state_all = more[:, 128:384]
    gate_up_all = own_half(rows_back(more[:, 384:512], gate_up))
    w_in_step_all = own_half(more[:, 512 : 512 + w_in_step.shape[1]])
    tiny_all = more[:, 640:].reshape(n_dp, -1, 128)[:, : tiny_pack.shape[0]]
    (
        gain_mlp_all,
        gain_mamba_all,
        conv_main_all,
        conv_main_bias_all,
        conv_state_all,
        conv_state_bias_all,
        gain_gated_all,
    ) = unpack(tiny_all, tiny_shapes)
    gain_mlp_all, gain_mamba_all = gain_mlp_all.reshape(-1), gain_mamba_all.reshape(-1)
    (
        conv_main_all,
        conv_main_bias_all,
        conv_state_all,
        conv_state_bias_all,
        gain_gated_all,
    ) = (
        rows_joined(me.restored(a, 0))
        for a in (
            conv_main_all,
            conv_main_bias_all,
            conv_state_all,
            conv_state_bias_all,
            gain_gated_all,
        )
    )
    conv_main_all = own_half(conv_main_all, 0).astype(f32)
    conv_main_bias_all = own_half(conv_main_bias_all, 0).astype(f32)
    gain_gated_f = own_half(gain_gated_all, 0).astype(f32)
    even = D // n_dp % 128 == 0
    order_d = me.columns_ordered(D) if even else [(0, D, 0)]
    hidden_shard, teacher_mid_shard, teacher_out_shard = move(
        [hidden, teacher_mid, teacher_out],
        [me.tensor * quarter],
        [(0, quarter)] * 3,
        [(i, c, w, i, None, to) for i in range(3) for c, w, to in order_d],
        [(quarter, D)] * 3,
    )
    if not even:
        hidden_shard = me.ordered(hidden_shard, 1)
        teacher_mid_shard = me.ordered(teacher_mid_shard, 1)
        teacher_out_shard = me.ordered(teacher_out_shard, 1)

    both = jnp.where(z == 0, jnp.stack([marks, marks_other], 1), jnp.stack([marks_other, marks], 1))
    segments, positions = both[0], both[1]
    marks_laid = (segments.reshape(T, 1), segments.reshape(2, 1, S))
    count = me.sum_everywhere(
        jnp.broadcast_to(jnp.sum(valid_mask.astype(f32)), (8, 128)), tensor=False
    )[0, 0]
    half = HEAD_SIZE // 2
    inverse = 10000.0 ** (-jnp.arange(half, dtype=f32) / half)
    angles = positions.reshape(T, 1).astype(f32) * inverse
    cosine = jnp.concatenate([jnp.cos(angles)] * 2, 1)
    sine = jnp.concatenate([-jnp.sin(angles), jnp.sin(angles)], 1)

    cat_shard = own_rows(own_cat).astype(f32)
    _, cat_back = jax.vjp(rms_scale, cat_shard, gain_attn_f)
    normed_other = me.gather_own(normed_came)
    normed_cat = place(
        [normed_own, normed_other], [z * S, (1 - z) * S], 0, T, me.columns_ordered(2 * D)
    )
    normed_cat_shard = own_tokens(normed_cat)
    normed_cat = me.after(normed_cat, "attn_out.far", "late.pair")
    query_low = narrow(times_right(normed_cat, query_down_all))
    query_pre = times_right(normed_cat, w_query_all) + times_right(query_low, query_up_all)
    key_pre = times_right(normed_cat, w_key_all)
    value_low = times_right(normed_cat, w_value_all, jnp.bfloat16)
    query_rot, key_rot, attended_low = attend_forward(
        query_pre, key_pre, value_low, cosine, sine, marks_laid
    )
    w_gate_up = me.near_gather(me.finish_line("gate_up", gate_up_line, hold=attended_low))
    down_line, in_line = me.finish_line(
        "late", late_line, [units + w_proj.shape[1] // 2, 3 * channels]
    )
    w_down_proj = me.near_gather(down_line)
    w_in_out = me.near_gather(in_line)
    w_down_all = w_down_proj[:, :units]
    w_proj_all = w_down_proj[:, units:]
    w_in_all = w_in_out[:, : 2 * channels]
    w_mamba_out_all = w_in_out[:, 2 * channels :]
    attended_low = me.after(attended_low, "gate_up.line")
    attn_part = times_trans(attended_low, w_attn_out_all, jnp.bfloat16)
    attn_shard = me.reduce_tokens(attn_part)

    hidden_shard = hidden_shard.astype(f32)
    first_sum = hidden_shard + attn_shard
    normed_mid_f, mid_back = jax.vjp(rms_scale, first_sum, gain_mlp_all.astype(f32))
    normed_mid_shard = narrow(normed_mid_f)
    normed_mid = me.gather_tokens(me.after(normed_mid_shard, "late.line"))
    gate_low = narrow(times_right(normed_mid, gate_down_all))
    gate_up_pre = times_right(normed_mid, w_gate_up)
    gate_pre = gate_up_pre[:, :units] + times_right(gate_low, gate_up_all)
    up_pre = gate_up_pre[:, units:]
    inner, inner_back = jax.vjp(gelu_product, gate_pre, up_pre)
    inner = narrow(inner)
    mlp_part = narrow(
        times_trans(w_down_all, inner) + times_trans(w_attn_out_all, attended_low)
    )
    shared_out = narrow(me.reduce_features(mlp_part))
    projected = me.reduce_tokens(
        narrow(
            lax.dot_general(
                shared_out, w_proj_all, (((0,), (1,)), ((), ())), preferred_element_type=f32
            )
        )
    )
    middle = hidden_shard + projected

    normed_last_f, last_back = jax.vjp(rms_scale, middle, gain_mamba_all.astype(f32))
    normed_last_shard = narrow(normed_last_f)
    normed_last = me.gather_tokens(normed_last_shard)
    mamba_in = times_right(normed_last, w_in_all)
    mamba_gate = mamba_in[:, :channels].reshape(2, S, channels)
    mamba_pre = mamba_in[:, channels:].reshape(2, S, channels)
    state_pre = times_right(normed_last, w_in_state_all).reshape(2, S, 2 * STATE)
    mamba_here = w_in_step_all.shape[1]
    step_pre = times_right(normed_last, w_in_step_all).reshape(2, S, mamba_here)
    convolve = partial(conv_act, segments=segments)
    mamba_act, main_conv_back = jax.vjp(convolve, mamba_pre, conv_main_all, conv_main_bias_all)
    state_act, state_conv_back = jax.vjp(
        convolve, state_pre, conv_state_all.astype(f32), conv_state_bias_all.astype(f32)
    )
    state_in = narrow(state_act[..., :STATE])
    state_out = narrow(state_act[..., STATE:])
    (accum, step_sizes), decay_back = jax.vjp(
        decay_piece,
        step_pre,
        own_half(step_bias, 0).astype(f32),
        own_half(decay_log, 0).astype(f32),
    )
    sizes_down, _ = by_heads(step_sizes)
    accum_down, accum_across = by_heads(accum)
    act_flat = mamba_act.reshape(T, channels)
    in_flat, out_flat = state_in.reshape(T, STATE), state_out.reshape(T, STATE)
    mix_inputs = (act_flat, sizes_down, accum_down, accum_across, in_flat, out_flat, marks_laid)
    core = mix_forward(*mix_inputs).reshape(2, S, channels)
    mixed, mixed_back = jax.vjp(
        mixed_piece, core, mamba_act, mamba_gate, own_half(skip_scale, 0).astype(f32)
    )
    square_part = jnp.sum(mixed * mixed, axis=-1).reshape(2, 2, 2, 1, quarter)
    square_total = me.halve(square_part, "zxc", "cxz", f32).reshape(quarter)
    scaled = narrow(mixed * gain_gated_f).reshape(T, channels)
    mamba_sum = me.reduce_tokens(times_trans(scaled, w_mamba_out_all, jnp.bfloat16))
    inverse_rms = lax.rsqrt(square_total / DI + eps)[:, None]
    mamba_branch = inverse_rms * mamba_sum
    final_sum = middle + mamba_branch

    valid_rows = own_rows(valid_mask).astype(f32)[:, None]
    miss_mid = middle - teacher_mid_shard.astype(f32)
    miss_out = final_sum - teacher_out_shard.astype(f32)
    square_mid = jnp.sum(valid_rows * miss_mid * miss_mid)
    square_out = jnp.sum(valid_rows * miss_out * miss_out)
    factor = S * n_dp / count
    grad_final = factor * valid_rows * miss_out
    row_inner = jnp.sum(grad_final * mamba_branch, axis=-1)
    pull = row_inner * inverse_rms[:, 0] * inverse_rms[:, 0] / DI
    branch_grad = me.gather_tokens(narrow(inverse_rms * grad_final))
    pull_all = me.gather_small(pull).reshape(2, S, 1)

    dw_mamba_out = trans_times(branch_grad, scaled, jnp.bfloat16)
    sum_mamba_out = me.square_sum(dw_mamba_out)
    grad_scaled = times_right(branch_grad, w_mamba_out_all).reshape(2, S, channels)
    grad_gain_gated = jnp.sum(grad_scaled * mixed, axis=(0, 1))
    grad_mixed = grad_scaled * gain_gated_f - mixed * pull_all
    grad_core, grad_heads, grad_gate_z, grad_skip_scale = mixed_back(grad_mixed)
    act_part, dsize, gram_grad, dacc, dturned = mix_backward(
        narrow(grad_core).reshape(T, channels), *mix_inputs
    )

    def from_down(values):
        return values.transpose(0, 2, 1, 3).reshape(2, S, mamba_here)

    grad_accum = from_down(dacc) - dturned.reshape(2, mamba_here, S).transpose(0, 2, 1)
    grad_step_pre, grad_step_bias, grad_decay_log = decay_back((grad_accum, from_down(dsize)))
    grad_heads = grad_heads + act_part.reshape(2, S, channels)
    grad_state_part = jnp.concatenate(
        [
            jnp.einsum("bts,bte->bse", gram_grad, state_out, preferred_element_type=f32),
            jnp.einsum("bts,bse->bte", gram_grad, state_in, preferred_element_type=f32),
        ],
        axis=-1,
    )
    state_shard = me.reduce_tokens(narrow(grad_state_part).reshape(T, 2 * STATE))
    grad_state = me.gather_tokens(narrow(state_shard)).astype(f32).reshape(2, S, 2 * STATE)
    grad_mamba_pre, grad_conv_main, grad_conv_main_bias = main_conv_back(
        grad_heads.reshape(2, S, channels)
    )
    grad_in = jnp.concatenate([narrow(grad_gate_z), narrow(grad_mamba_pre)], -1).reshape(T, -1)
    step_grad_low = narrow(grad_step_pre).reshape(T, -1)
    sum_in = me.square_sum(trans_times(normed_last, grad_in, jnp.bfloat16))
    grad_w_in_step = me.restored(trans_times(normed_last, step_grad_low, jnp.bfloat16), 0)
    last_part = times_trans(grad_in, w_in_all) + times_trans(step_grad_low, w_in_step_all)
    last_part = lax.optimization_barrier((narrow(last_part), sum_mamba_out))[0]
    last_shard = me.reduce_tokens(last_part)
    grad_state_pre, grad_conv_state, grad_conv_state_bias = state_conv_back(grad_state)
    state_grad_low = own_tokens(narrow(grad_state_pre).reshape(T, -1))
    grad_w_in_state = trans_times(normed_last_shard, state_grad_low, jnp.bfloat16)
    grad_middle, grad_gain_mamba = last_back(
        last_shard + times_trans(state_grad_low, w_in_state_all)
    )
    grad_middle = grad_middle + grad_final + factor * valid_rows * miss_mid

    projected_grad = me.gather_tokens(narrow(grad_middle))
    sum_proj = me.near_sum(
        narrow(
            lax.dot_general(
                projected_grad, shared_out, (((0,), (1,)), ((), ())), preferred_element_type=f32
            )
        )
    )
    mlp_grad = me.gather_features(times_right(projected_grad, w_proj_all, jnp.bfloat16))
    mlp_grad = lax.optimization_barrier((mlp_grad, sum_in))[0]
    dw_down = trans_times(mlp_grad, inner, jnp.bfloat16)
    sum_down = me.near_sum(dw_down)
    grad_gate_pre, grad_up_pre = inner_back(times_right(mlp_grad, w_down_all))
    gate_grad = narrow(grad_gate_pre)
    up_grad = narrow(grad_up_pre)
    pre_grad = jnp.concatenate([gate_grad, up_grad], 1)
    dw_gate_up = trans_times(normed_mid, pre_grad, jnp.bfloat16)
    sum_gate_up = me.near_sum(dw_gate_up)
    mid_part = times_trans(pre_grad, w_gate_up, jnp.bfloat16)
    mid_part = lax.optimization_barrier((mid_part, dw_down, dw_gate_up))[0]
    low_part = times_trans(gate_grad, gate_up_all, jnp.bfloat16)
    mid_shard = me.reduce_tokens(mid_part)
    gate_low_grad = narrow(me.reduce_tokens(low_part))
    grad_w_gate, grad_w_up = me.scatter_unit("gate_up", sum_gate_up, parts=(2,))
    grad_gate_up = trans_times(gate_low, gate_grad, jnp.bfloat16)
    grad_gate_down = trans_times(normed_mid_shard, gate_low_grad, jnp.bfloat16)
    grad_first, grad_gain_mlp = mid_back(mid_shard + times_trans(gate_low_grad, gate_down_all))

    attn_grad_shard = narrow(own_tokens(mlp_grad).astype(f32) + grad_first)
    attn_grad = me.gather_tokens(attn_grad_shard)
    sum_attn_out = me.near_sum(trans_times(attn_grad, attended_low, jnp.bfloat16))
    attended_grad = times_right(attn_grad, w_attn_out_all, jnp.bfloat16)
    attended_grad = me.after(attended_grad, "gate_up.ready")
    query_grad, key_grad, value_grad = attend_backward(
        query_rot, key_rot, value_low, attended_grad, cosine, sine, marks_laid
    )
    sum_value = me.near_sum(trans_times(normed_cat, value_grad, jnp.bfloat16))
    sum_key = me.near_sum(trans_times(normed_cat, key_grad, jnp.bfloat16))
    sum_query = me.near_sum(trans_times(normed_cat, query_grad, jnp.bfloat16))
    cat_part = narrow(
        times_trans(query_grad, w_query_all)
        + times_trans(key_grad, w_key_all)
        + times_trans(value_grad, w_value_all)
    )
    low_part = times_trans(query_grad, query_up_all, jnp.bfloat16)
    cat_part = me.after(cat_part, "gate_up.sum")
    cat_shard_sum = me.reduce_tokens(cat_part)
    query_low_grad = narrow(me.reduce_tokens(low_part))
    def later(values):
        return lax.optimization_barrier((values, cat_shard_sum))[0]

    grad_w_proj, grad_w_down = me.scatter_unit("block", later(sum_proj), later(sum_down))
    (grad_w_attn_out,) = me.scatter_unit("d_attn_out", later(sum_attn_out))
    (grad_w_value,) = me.scatter_unit("d_value", later(sum_value))
    (grad_w_key,) = me.scatter_unit("key", sum_key)
    (grad_w_query,) = me.scatter_unit("query", sum_query)
    grad_w_mamba_out, grad_w_in_gate, grad_w_in_main = me.join_halves(
        "mixer", later(sum_mamba_out), later(sum_in), parts=(1, 2)
    )
    grad_query_up = trans_times(query_low, query_grad, jnp.bfloat16)
    grad_query_down = trans_times(normed_cat_shard, query_low_grad, jnp.bfloat16)
    grad_concat, grad_gain_attn = cat_back(
        me.restored_rows(cat_shard_sum + times_trans(query_low_grad, query_down_all))
    )
    stream = me.restored_rows(grad_first + grad_middle)
    grad_both = jnp.concatenate([grad_concat[:, :D] + stream, grad_concat[:, D:]], 1)
    grad_both = me.gather_own(narrow(grad_both)).astype(f32)
    if even:
        final_low = lax.optimization_barrier((narrow(final_sum), cat_part))[0]
        output = me.gather_own(final_low, me.columns_restored(D))
    else:
        output = me.gather_own(me.restored(narrow(final_sum), 1))

    def by_dp(values):
        return values.reshape((n_dp, values.shape[0] // n_dp) + values.shape[1:])

    def both_halves(values, axis):
        axis = axis % values.ndim
        nothing = jnp.zeros_like(values)
        return jnp.where(
            z == 0,
            jnp.concatenate([values, nothing], axis),
            jnp.concatenate([nothing, values], axis),
        )

    first = (me.tensor == 0) & (z == 0)
    shared = (
        me.restored(grad_gain_mlp, 0),
        me.restored(grad_gain_mamba, 0),
        jnp.where(first, grad_conv_state, 0.0),
        jnp.where(first, grad_conv_state_bias, 0.0),
        me.restored(grad_gate_down, 0),
        me.restored(grad_w_in_state, 0),
    )
    shared_out_shapes = (
        gain_mlp.shape,
        gain_mamba.shape,
        conv_state.shape,
        conv_state_bias.shape,
        gate_down.shape,
        w_in_state.shape,
    )
    shared += (grad_gain_attn, me.restored(grad_query_down, 0))
    shared_out_shapes += (gain_attn.shape, query_down.shape)
    split = (
        both_halves(grad_conv_main, 0),
        both_halves(grad_conv_main_bias, 0),
        both_halves(grad_gain_gated, 0),
        both_halves(grad_gate_up, 1),
        both_halves(grad_w_in_step, 1),
        both_halves(grad_query_up, 1),
    )
    split_shapes = (
        conv_main.shape,
        conv_main_bias.shape,
        gain_gated.shape,
        gate_up.shape,
        w_in_step.shape,
        query_up.shape,
    )
    shared_rows = pack([by_dp(narrow(a)) for a in shared], n_dp)
    part_rows = shared_rows.shape[1] // 4
    blocks = shared_rows.reshape(n_dp, 2, 2, part_rows, 128).transpose(1, 2, 0, 3, 4)
    shared_mine = narrow(me.halve(blocks, "xc", "cx"))
    split_rows = pack([by_dp(narrow(a)) for a in split], n_dp)
    small_mine = me.sum_dp(rows_joined(jnp.concatenate([shared_mine, split_rows], 1)))
    shared_sum = me.gather_own(small_mine[:part_rows])
    (
        out_gain_mlp,
        out_gain_mamba,
        out_conv_state,
        out_conv_state_bias,
        out_gate_down,
        out_w_in_state,
        out_gain_attn,
        out_query_down,
    ) = [v[0].astype(f32) for v in unpack(shared_sum[None], shared_out_shapes)]
    (
        out_conv_main,
        out_conv_main_bias,
        out_gain_gated,
        out_gate_up,
        out_w_in_step,
        out_query_up,
    ) = [v[0].astype(f32) for v in unpack(small_mine[None, part_rows:], split_shapes)]
    grad_step_bias, grad_decay_log, grad_skip_scale, square_mid, square_out = (
        lax.optimization_barrier(
            (grad_step_bias, grad_decay_log, grad_skip_scale, square_mid, square_out, cat_part)
        )[:5]
    )
    head_rows = jnp.stack(
        [
            both_halves(grad_step_bias, 0),
            both_halves(grad_decay_log, 0),
            both_halves(grad_skip_scale, 0),
        ]
    )
    head_sums = me.sum_everywhere(head_rows, tensor=False)
    losses = me.sum_everywhere(
        jnp.stack(
            [jnp.broadcast_to(square_mid, (128,)), jnp.broadcast_to(square_out, (128,))]
        )
    )
    loss_mid = losses[0, 0] / (count * D)
    loss_out = losses[1, 0] / (count * D)
    return (
        output,
        loss_mid,
        loss_out,
        grad_both[:, :D],
        grad_both[:, D:],
        out_gain_attn,
        grad_w_query,
        grad_w_key,
        grad_w_value,
        out_query_down,
        out_query_up,
        grad_w_attn_out,
        out_gain_mlp,
        grad_w_gate,
        grad_w_up,
        out_gate_down,
        out_gate_up,
        grad_w_down,
        grad_w_proj,
        out_gain_mamba,
        grad_w_in_gate,
        grad_w_in_main,
        out_w_in_state,
        out_w_in_step,
        out_conv_main,
        out_conv_main_bias,
        out_conv_state,
        out_conv_state_bias,
        out_gain_gated,
        grad_w_mamba_out,
        head_sums[0],
        head_sums[1],
        head_sums[2],
    )


def solution(mesh):
    in_specs = (
        P("dp", None),
        P("dp", None),
        P("dp", None),
        P("dp", None),
        P("dp"),
        P("dp"),
        P("dp"),
        P("dp"),
        P("dp", "tensor"),
        P("dp", "tensor"),
        P("dp", "tensor"),
        P("dp", None),
        P("dp", "tensor"),
        P("dp", "tensor"),
        P("dp"),
        P("dp", "tensor"),
        P("dp", "tensor"),
        P("dp", None),
        P("dp", "tensor"),
        P("dp", "tensor"),
        P("dp", "tensor"),
        P("dp"),
        P("dp", "tensor"),
        P("dp", "tensor"),
        P("dp", None),
        P("dp", "tensor"),
        P(("tensor", "dp"), None),
        P(("tensor", "dp")),
        P("dp", None),
        P("dp"),
        P(("tensor", "dp")),
        P("dp", "tensor"),
        P("tensor"),
        P("tensor"),
        P("tensor"),
    )
    out_specs = (
        P("dp", None),
        P(),
        P(),
        P("dp", None),
        P("dp", None),
        P("dp"),
        P("dp", "tensor"),
        P("dp", "tensor"),
        P("dp", "tensor"),
        P("dp", None),
        P("dp", "tensor"),
        P("dp", "tensor"),
        P("dp"),
        P("dp", "tensor"),
        P("dp", "tensor"),
        P("dp", None),
        P("dp", "tensor"),
        P("dp", "tensor"),
        P("dp", "tensor"),
        P("dp"),
        P("dp", "tensor"),
        P("dp", "tensor"),
        P("dp", None),
        P("dp", "tensor"),
        P(("tensor", "dp"), None),
        P(("tensor", "dp")),
        P("dp", None),
        P("dp"),
        P(("tensor", "dp")),
        P("dp", "tensor"),
        P("tensor"),
        P("tensor"),
        P("tensor"),
    )
    return jax.shard_map(body, mesh=mesh, in_specs=in_specs, out_specs=out_specs, check_vma=False)
```

```python
from functools import partial

import jax
import jax.numpy as jnp
from jax import lax
from jax.experimental import pallas as pl
from jax.experimental.pallas import tpu as pltpu
from jax.sharding import PartitionSpec as P

D = 2048
HEAD_SIZE = 128
STATE = 128
DI = 4096
HEAD_M = 64
PAIR = 2

eps = 1e-05
f32 = jnp.float32


def narrow(values):
    return values.astype(jnp.bfloat16)


def times_right(left, right, out=f32):
    return jnp.dot(left, right, preferred_element_type=f32).astype(out)


def times_trans(left, right, out=f32):
    return lax.dot_general(
        left, right, (((1,), (1,)), ((), ())), preferred_element_type=f32
    ).astype(out)


def trans_times(left, right, out=f32):
    return lax.dot_general(
        left, right, (((0,), (0,)), ((), ())), preferred_element_type=f32
    ).astype(out)


def rms_scale(values, gain):
    return values * lax.rsqrt(jnp.mean(values * values, axis=-1, keepdims=True) + eps) * gain


def flip(values, axis, bit):
    count = lax.axis_size(axis)
    return lax.ppermute(values, axis, [(i, i ^ bit) for i in range(count)])


def pick(values, axis, index):
    return lax.dynamic_index_in_dim(values, index, axis, keepdims=False)


def move_kernel(loads, stores, n_in, n_out, at_ref, *refs):
    ins, outs = refs[:n_in], refs[n_in : n_in + n_out]
    rooms, came, left = refs[n_in + n_out : -2], refs[-2], refs[-1]
    arrivals = []
    for i, (row, rows) in enumerate(loads):
        source = ins[i]
        if row is not None:
            source = source.at[pl.ds(pl.multiple_of(at_ref[row], rows), rows)]
        arrivals.append(pltpu.make_async_copy(source, rooms[i], came.at[i]))
        arrivals[-1].start()
    waiting, seen = [], set()
    for k, (i, column, width, out, row, to) in enumerate(stores):
        if i not in seen:
            arrivals[i].wait()
            seen.add(i)
        source = rooms[i].at[:, column : column + width]
        rows = loads[i][1]
        target = outs[out]
        if row is not None:
            target = target.at[pl.ds(pl.multiple_of(at_ref[row], rows), rows)]
        if isinstance(to, tuple):
            target = target.at[:, pl.ds(pl.multiple_of(at_ref[to[0]], width), width)]
        else:
            target = target.at[:, to : to + width]
        waiting.append(pltpu.make_async_copy(source, target, left.at[k]))
        waiting[-1].start()
    for store in waiting:
        store.wait()


def move(pieces, at, loads, stores, shapes):
    dtype = pieces[0].dtype
    at = jnp.stack(at).astype(jnp.int32) if at else jnp.zeros((1,), jnp.int32)
    return pl.pallas_call(
        partial(move_kernel, tuple(loads), tuple(stores), len(pieces), len(shapes)),
        out_shape=[jax.ShapeDtypeStruct(shape, dtype) for shape in shapes],
        in_specs=[pl.BlockSpec(memory_space=pltpu.SMEM)]
        + [pl.BlockSpec(memory_space=pl.ANY)] * len(pieces),
        out_specs=[pl.BlockSpec(memory_space=pl.ANY)] * len(shapes),
        scratch_shapes=[
            pltpu.VMEM((load[1], piece.shape[1]), dtype) for load, piece in zip(loads, pieces)
        ]
        + [pltpu.SemaphoreType.DMA((len(pieces),)), pltpu.SemaphoreType.DMA((len(stores),))],
    )(at, *pieces)


def place(pieces, starts, along, total, columns=None, widths=None):
    shape = list(pieces[0].shape)
    wide = shape[1]
    shape[along] = total
    if widths is not None:
        stores = []
        for i in range(len(pieces)):
            first = 0
            for out, width in enumerate(widths):
                stores.append((i, first, width, out, i, 0))
                first += width
        loads = [(None, piece.shape[0]) for piece in pieces]
        return move(pieces, starts, loads, stores, [(total, width) for width in widths])
    columns = columns or [(0, wide, 0)]
    stores = []
    for i in range(len(pieces)):
        for first, width, to in columns:
            if along == 0:
                stores.append((i, first, width, 0, i, to))
            else:
                stores.append((i, 0, wide, 0, None, (i,)))
    loads = [(None, piece.shape[0]) for piece in pieces]
    return move(pieces, starts, loads, stores, [tuple(shape)])[0]


class Place:
    def __init__(self):
        self.dp = lax.axis_index("dp")
        self.tensor = lax.axis_index("tensor")
        self.n_dp = lax.axis_size("dp")
        self.z = (self.dp // PAIR) % 2
        self.x = self.tensor // 2
        self.c = self.tensor % 2
        bits = [1 << k for k in range(self.n_dp.bit_length() - 1)]
        self.dp_bits = bits
        self.far_bits = [b for b in bits if b not in (1, PAIR)]
        self.pairs = [[i, i + 1] for i in range(0, self.n_dp, 2)]
        self.square = [
            [y + PAIR * z + 4 * far for y in (0, 1) for far in range(self.n_dp // 4)]
            for z in (0, 1)
        ]
        self.gates = {"pair": [], "far": []}
        self.marks = {}

    def dp_bit(self, bit):
        return (self.dp // bit) % 2


    def half(self, shard, which):
        width = shard.shape[1] // 2
        return lax.dynamic_slice_in_dim(shard, which * width, width, 1)

    def send(self, values, bit):
        gate = self.gates["pair" if bit == PAIR else "far"]
        if gate:
            values = lax.optimization_barrier((values, *gate))[0]
        came = flip(values, "dp", bit)
        gate[:] = [came]
        return came

    def blocks(self, values, axis, order):
        size = values.shape[axis] // self.n_dp
        parts = [lax.slice_in_dim(values, i * size, (i + 1) * size, axis=axis) for i in order]
        return jnp.concatenate(parts, axis)

    def ordered(self, values, axis):
        order = [i for low in (0, 1) for i in range(low, self.n_dp, 2)]
        return self.blocks(values, axis, order)

    def restored(self, values, axis):
        half = self.n_dp // 2
        return self.blocks(values, axis, [i // 2 + half * (i % 2) for i in range(self.n_dp)])

    def columns_ordered(self, wide, first=0):
        size, half = wide // self.n_dp, self.n_dp // 2
        return [
            (first + i * size, size, (i % 2 * half + i // 2) * size) for i in range(self.n_dp)
        ]

    def columns_restored(self, wide):
        return [(to, size, first) for first, size, to in self.columns_ordered(wide)]

    def restored_rows(self, values):
        rows, wide = values.shape
        if wide // self.n_dp % 128:
            return self.restored(values, 1)
        stores = [(0, c, w, 0, None, to) for c, w, to in self.columns_restored(wide)]
        return move([values], [], [(None, rows)], stores, [values.shape])[0]

    def after(self, values, *names):
        return lax.optimization_barrier((values, *(self.marks[n] for n in names)))[0]

    def halves(self, shards, extra=()):
        mine = jnp.concatenate([*(self.half(s, self.z) for s in shards), *extra], 1)
        partner = jnp.concatenate([*(self.half(s, 1 - self.z) for s in shards), *extra], 1)
        return mine, partner

    def near_gather(self, line):
        return lax.all_gather(line, "dp", axis=0, tiled=True, axis_index_groups=self.pairs)

    def swap(self, *shards, extra=()):
        mine, partner = self.halves(shards, extra)
        return mine, self.send(partner, PAIR)

    def gather_weight(self, mine, came, *early):
        pieces = {0: mine, PAIR: came}
        for bit in self.far_bits:
            for mask in list(pieces):
                pieces[mask | bit] = self.send(pieces[mask], bit)
        rows = mine.shape[0]
        starts = [((self.dp ^ mask) // 2) * rows for mask in pieces]
        line = place(list(pieces.values()), starts, 0, self.n_dp // 2 * rows)
        self.gates["far"] += [line, *early]
        return self.near_gather(line)

    def start_line(self, name, mine, came, widths=None):
        rows = mine.shape[0]
        starts = [self.z * rows, (1 - self.z) * rows]
        line = place([mine, came], starts, 0, 2 * rows, widths=widths)
        self.marks[name + ".pair"] = line if widths is None else line[0]
        return line

    def finish_line(self, name, line, widths=None, hold=None):
        for bit in self.far_bits:
            rows = line.shape[0]
            came = self.send(line, bit)
            if hold is not None:
                came = lax.optimization_barrier((came, hold))[0]
            own = self.dp_bit(bit)
            cut = widths if bit == self.far_bits[-1] else None
            line = place([line, came], [own * rows, (1 - own) * rows], 0, 2 * rows, widths=cut)
        self.marks[name + ".far"] = came
        self.marks[name + ".line"] = line if widths is None else line[0]
        return line

    def gather_packed(self, packed):
        value = packed[None]
        for bit in [PAIR] + self.far_bits:
            other = flip(value, "dp", bit)
            low = self.dp_bit(bit) == 0
            value = jnp.concatenate(
                [jnp.where(low, value, other), jnp.where(low, other, value)]
            )
        other = flip(value, "dp", 1)
        value = jnp.where(
            self.dp % 2 == 0, jnp.stack([value, other], 1), jnp.stack([other, value], 1)
        )
        return value.reshape((-1,) + packed.shape)

    def split_dp(self, values):
        rows = values.shape[0] // self.n_dp
        return values.reshape((2,) * len(self.dp_bits) + (rows,) + values.shape[1:])

    def sum_dp(self, values):
        values = self.split_dp(values)
        for k, bit in enumerate(reversed(self.dp_bits)):
            mine = self.dp_bit(bit)
            away = narrow(pick(values, 0, 1 - mine))
            kept = pick(values, 0, mine).astype(f32)
            values = narrow(kept + flip(away, "dp", bit).astype(f32))
        return values

    def near_sum(self, grad):
        return lax.psum_scatter(
            grad, "dp", scatter_dimension=0, tiled=True, axis_index_groups=self.pairs
        )

    def square_sum(self, grad):
        return lax.psum_scatter(
            grad, "dp", scatter_dimension=0, tiled=True, axis_index_groups=self.square
        )

    def join_halves(self, name, *summed, parts=None):
        values = [v.reshape(2, v.shape[0] // 2, v.shape[1]) for v in summed]
        return self.join(name, values, parts)

    def scatter_unit(self, name, *summed, parts=None):
        rows = 2 * summed[0].shape[0] // self.n_dp
        left = [b for b in reversed(self.dp_bits) if b != 1]
        values = [v.reshape((2,) * len(left) + (rows, v.shape[1])) for v in summed]
        for bit in self.far_bits:
            at = left.index(bit)
            mine = self.dp_bit(bit)
            away = jnp.concatenate([pick(v, at, 1 - mine) for v in values], -1)
            if bit == self.far_bits[0]:
                self.marks[name + ".ready"] = away
            came = self.send(away, bit)
            first, added = 0, []
            for v in values:
                width = v.shape[-1]
                part = came[..., first : first + width].astype(f32)
                added.append(narrow(pick(v, at, mine).astype(f32) + part))
                first += width
            values = added
            left.pop(at)
        self.marks[name + ".sum"] = came
        return self.join(name, values, parts)

    def join(self, name, values, parts):
        away = jnp.concatenate([pick(v, 0, 1 - self.z) for v in values], -1)
        self.marks[name + ".turn"] = away
        other = self.send(away, PAIR)
        self.marks[name + ".swap"] = other
        out, first = [], 0
        for v, count in zip(values, parts or (1,) * len(values)):
            mine = pick(v, 0, self.z)
            width = v.shape[-1] // count
            for i in range(count):
                a = mine[:, i * width : (i + 1) * width]
                b = other[:, first : first + width]
                joined = jnp.where(
                    self.z == 0, jnp.concatenate([a, b], 1), jnp.concatenate([b, a], 1)
                )
                out.append(joined.astype(f32))
                first += width
        return out


    def hop(self, values, name):
        if name == "z":
            return flip(values, "dp", PAIR)
        return flip(values, "tensor", 2 if name == "x" else 1)

    def halve(self, values, order, names, kind=jnp.bfloat16):
        order = list(order)
        for name in names:
            at = order.index(name)
            mine = getattr(self, name)
            away = pick(values, at, 1 - mine).astype(kind)
            kept = pick(values, at, mine).astype(f32)
            values = kept + self.hop(away, name).astype(f32)
            order.pop(at)
            if order:
                values = values.astype(kind)
        return values

    def reduce_tokens(self, part):
        rows, wide = part.shape
        blocks = part.reshape(2, 2, 2, rows // 8, wide)
        first = self.halve(blocks, "zxc", "c")
        cut = wide // 2
        return jnp.concatenate(
            [
                self.halve(narrow(first)[..., :cut], "zx", "xz"),
                self.halve(narrow(first)[..., cut:], "zx", "zx"),
            ],
            -1,
        )

    def reduce_features(self, part):
        if self.n_dp != 8:
            wide, rows = part.shape
            part = self.restored(part, 0).reshape(2, 2, 2, wide // 8, rows)
            part = part.transpose(2, 0, 1, 3, 4).reshape(wide, rows)
        return self.reduce_tokens(part)

    def spread(self, shard, cut_at):
        by_z = self.hop(shard, "z")
        by_x = self.hop(shard, "x")
        far_a = self.hop(by_z[:cut_at], "x")
        far_b = self.hop(by_x[cut_at:], "z")
        pieces = [(0, 0, None, shard), (1, 0, None, by_z), (0, 1, None, by_x)]
        pieces += [(1, 1, 0, far_a), (1, 1, 1, far_b)]
        out = []
        for dz, dx, part, piece in pieces:
            out.append((dz, dx, 0, part, piece))
            out.append((dz, dx, 1, part, self.hop(piece, "c")))
        return out

    def gather_tokens(self, shard):
        rows = shard.shape[0]
        pieces, starts = [], []
        for dz, dx, dc, part, piece in self.spread(shard, rows // 2):
            block = (self.z ^ dz) * 4 + (self.x ^ dx) * 2 + (self.c ^ dc)
            starts.append(block * rows + (rows // 2 if part == 1 else 0))
            pieces.append(piece)
        return place(pieces, starts, 0, 8 * rows)

    def gather_features(self, shard):
        wide = shard.shape[1]
        by_z = self.hop(shard, "z")
        by_x = self.hop(shard, "x")
        far = self.hop(by_z, "x")
        pieces, starts = [], []
        for dz, dx, piece in ((0, 0, shard), (1, 0, by_z), (0, 1, by_x), (1, 1, far)):
            for dc, value in ((0, piece), (1, self.hop(piece, "c"))):
                block = (self.x ^ dx) * 4 + (self.c ^ dc) * 2 + (self.z ^ dz)
                if self.n_dp == 8:
                    block = block % 2 * 4 + block // 2
                starts.append(block * wide)
                pieces.append(value)
        whole = place(pieces, starts, 1, 8 * wide)
        return whole if self.n_dp == 8 else self.ordered(whole, 1)

    def gather_own(self, shard, columns=None):
        rows = shard.shape[0]
        by_x = self.hop(shard, "x")
        pieces, starts = [], []
        for dx, piece in ((0, shard), (1, by_x)):
            for dc, value in ((0, piece), (1, self.hop(piece, "c"))):
                starts.append(((self.x ^ dx) * 2 + (self.c ^ dc)) * rows)
                pieces.append(value)
        return place(pieces, starts, 0, 4 * rows, columns)

    def gather_small(self, row):
        value = row
        for name in "cxz":
            mine = getattr(self, name)
            other = self.hop(value, name)
            value = jnp.where(
                mine == 0,
                jnp.concatenate([value, other]),
                jnp.concatenate([other, value]),
            )
        return value

    def sum_everywhere(self, values, tensor=True):
        for bit in self.dp_bits:
            values = values + flip(values, "dp", bit)
        if tensor:
            for bit in (1, 2):
                values = values + flip(values, "tensor", bit)
        return values


def small_rows(size):
    return -(-size // 128)


def pack(arrays, lead):
    rows = []
    for a in arrays:
        flat = a.reshape(lead, -1)
        size = flat.shape[1]
        flat = jnp.pad(flat, ((0, 0), (0, small_rows(size) * 128 - size)))
        rows.append(flat.reshape(lead, -1, 128))
    total = sum(r.shape[1] for r in rows)
    fill = -total % 64
    if fill:
        rows.append(jnp.zeros((lead, fill, 128), arrays[0].dtype))
    return jnp.concatenate(rows, 1)


def unpack(packed, shapes):
    out, at = [], 0
    lead = packed.shape[0]
    for shape in shapes:
        size = 1
        for s in shape:
            size *= s
        rows = small_rows(size)
        part = packed[:, at : at + rows].reshape(lead, rows * 128)[:, :size]
        out.append(part.reshape((lead,) + tuple(shape)))
        at += rows
    return out


def rows_joined(values):
    return values.reshape((values.shape[0] * values.shape[1],) + values.shape[2:])


def conv_act(pre, weight, bias, segments):
    length = pre.shape[1]
    taps = weight.shape[1]
    total = jnp.zeros_like(pre) + bias
    for tap in range(taps):
        lag = taps - 1 - tap
        shifted = jnp.pad(pre, ((0, 0), (lag, 0), (0, 0)))[:, :length]
        earlier = jnp.pad(segments, ((0, 0), (lag, 0)), constant_values=-1)[:, :length]
        keeping = (earlier == segments).astype(f32)[:, :, None]
        total = total + weight[:, tap] * shifted * keeping
    return jax.nn.silu(total)


def gelu_product(gate_pre, up_pre):
    return jax.nn.gelu(gate_pre, approximate=True) * up_pre


def decay_piece(step_pre, step_bias, decay_log):
    sizes = jax.nn.softplus(step_pre + step_bias)
    return (jnp.cumsum(sizes * -jnp.exp(decay_log), axis=1), sizes)


def mixed_piece(core, mamba_act, mamba_gate, skip_scale):
    wide = jnp.broadcast_to(skip_scale[:, None], (skip_scale.shape[0], HEAD_M)).reshape(-1)
    with_skip = core + wide * mamba_act
    return with_skip * jax.nn.silu(mamba_gate)


def dot_nn(left, right):
    return jnp.dot(left, right, preferred_element_type=f32)


def dot_nt(left, right):
    return lax.dot_general(left, right, (((1,), (1,)), ((), ())), preferred_element_type=f32)


def dot_tn(left, right):
    return lax.dot_general(left, right, (((0,), (0,)), ((), ())), preferred_element_type=f32)


def same_document(down, across):
    shape = (down.shape[0], across.shape[1])
    later = lax.broadcasted_iota(jnp.int32, shape, 0) >= lax.broadcasted_iota(
        jnp.int32, shape, 1
    )
    return later & (down == across)


def turn(values, cosine, sine):
    return values * cosine + pltpu.roll(values, HEAD_SIZE // 2, 1) * sine


def attend_probabilities(query, key, kept):
    scores = jnp.where(kept, dot_nt(query, key) * HEAD_SIZE ** (-0.5), -1e30)
    raised = jnp.exp(scores - jnp.max(scores, axis=1, keepdims=True))
    return raised / jnp.sum(raised, axis=1, keepdims=True)


def attend_kernel(q_ref, k_ref, v_ref, cos_ref, sin_ref, down_ref, across_ref, qo, ko, out):
    cosine, sine = cos_ref[...], sin_ref[...]
    query = narrow(turn(q_ref[...], cosine, sine))
    key = narrow(turn(k_ref[...], cosine, sine))
    qo[...] = query
    ko[...] = key
    kept = same_document(down_ref[...], across_ref[...])
    probabilities = narrow(attend_probabilities(query, key, kept))
    out[...] = narrow(dot_nn(probabilities, v_ref[...]))


def attend_back_kernel(
    q_ref, k_ref, v_ref, g_ref, cos_ref, sin_ref, down_ref, across_ref, dq, dk, dv
):
    query, key, grad = q_ref[...], k_ref[...], g_ref[...]
    kept = same_document(down_ref[...], across_ref[...])
    probabilities = attend_probabilities(query, key, kept)
    dv[...] = narrow(dot_tn(narrow(probabilities), grad))
    grad_probs = dot_nt(grad, v_ref[...])
    inner = jnp.sum(probabilities * grad_probs, axis=1, keepdims=True)
    grad_scores = narrow(probabilities * (grad_probs - inner))
    cosine, sine = cos_ref[...], sin_ref[...]
    scale = HEAD_SIZE ** (-0.5)
    dq[...] = narrow(turn(dot_nn(grad_scores, key) * scale, cosine, -sine))
    dk[...] = narrow(turn(dot_tn(grad_scores, query) * scale, cosine, -sine))


def of_head(j):
    lane = lax.broadcasted_iota(jnp.int32, (1, 2 * HEAD_M), 1)
    return (lane >= j * HEAD_M) & (lane < (j + 1) * HEAD_M)


def decay_of(acc_ref, turned_ref, j, kept):
    lagged = acc_ref[:, j : j + 1] - turned_ref[j : j + 1, :]
    return jnp.where(kept, jnp.exp(jnp.where(kept, lagged, 0.0)), 0.0)


def weighted_of(act_ref, size_ref):
    return narrow(act_ref[...] * jnp.where(of_head(0), size_ref[:, 0:1], size_ref[:, 1:2]))


def mix_kernel(act_ref, size_ref, acc_ref, turned_ref, in_ref, out_ref, down_ref, across_ref, core):
    kept = same_document(down_ref[...], across_ref[...])
    gram = dot_nt(out_ref[...], in_ref[...])
    weighted = weighted_of(act_ref, size_ref)
    parts = [
        dot_nn(narrow(gram * decay_of(acc_ref, turned_ref, j, kept)), weighted) for j in (0, 1)
    ]
    core[...] = jnp.where(of_head(0), parts[0], parts[1])


def mix_back_kernel(
    grad_ref,
    act_ref,
    size_ref,
    acc_ref,
    turned_ref,
    in_ref,
    out_ref,
    down_ref,
    across_ref,
    dact,
    dsize,
    dgram,
    dacc,
    dturned,
    total,
):
    kept = same_document(down_ref[...], across_ref[...])
    gram = dot_nt(out_ref[...], in_ref[...])
    weighted = weighted_of(act_ref, size_ref)
    grad = grad_ref[...]

    @pl.when(pl.program_id(1) == 0)
    def _():
        total[...] = jnp.zeros_like(total)

    parts = []
    for j in (0, 1):
        decay = decay_of(acc_ref, turned_ref, j, kept)
        mixing = gram * decay
        parts.append(dot_tn(narrow(mixing), grad))
        grad_mixing = dot_nt(jnp.where(of_head(j), grad, jnp.zeros_like(grad)), weighted)
        total[...] += grad_mixing * decay
        grad_lag = grad_mixing * mixing
        dacc[:, j : j + 1] = jnp.sum(grad_lag, axis=1, keepdims=True)
        dturned[j : j + 1, :] = jnp.sum(grad_lag, axis=0, keepdims=True)
    grad_weighted = jnp.where(of_head(0), parts[0], parts[1])
    dact[...] = grad_weighted * jnp.where(of_head(0), size_ref[:, 0:1], size_ref[:, 1:2])
    product = grad_weighted * act_ref[...]
    for j in (0, 1):
        dsize[:, j : j + 1] = jnp.sum(
            jnp.where(of_head(j), product, 0.0), axis=1, keepdims=True
        )

    @pl.when(pl.program_id(1) == pl.num_programs(1) - 1)
    def _():
        dgram[...] = narrow(total[...])


def by_columns(S):
    return pl.BlockSpec((S, 128), lambda b, h: (b, h))


def by_sequence(S):
    return pl.BlockSpec((S, 128), lambda b, h: (b, 0))


def marks_specs(S):
    return [
        pl.BlockSpec((S, 1), lambda b, h: (b, 0)),
        pl.BlockSpec((None, 1, S), lambda b, h: (b, 0, 0)),
    ]


def attend_forward(query_pre, key_pre, value_low, cosine, sine, marks):
    T, wide = query_pre.shape
    S = T // 2
    low = jax.ShapeDtypeStruct((T, wide), jnp.bfloat16)
    return pl.pallas_call(
        attend_kernel,
        grid=(2, wide // 128),
        in_specs=[by_columns(S)] * 3 + [by_sequence(S)] * 2 + marks_specs(S),
        out_specs=[by_columns(S)] * 3,
        out_shape=[low] * 3,
    )(query_pre, key_pre, value_low, cosine, sine, *marks)


def attend_backward(query_rot, key_rot, value_low, grad, cosine, sine, marks):
    T, wide = query_rot.shape
    S = T // 2
    low = jax.ShapeDtypeStruct((T, wide), jnp.bfloat16)
    return pl.pallas_call(
        attend_back_kernel,
        grid=(2, wide // 128),
        in_specs=[by_columns(S)] * 4 + [by_sequence(S)] * 2 + marks_specs(S),
        out_specs=[by_columns(S)] * 3,
        out_shape=[low] * 3,
    )(query_rot, key_rot, value_low, grad, cosine, sine, *marks)


def by_heads(values):
    _, S, heads = values.shape
    turned = values.transpose(0, 2, 1).reshape(2, heads // 2, 2, S)
    return turned.transpose(0, 1, 3, 2), turned


def heads_specs(S):
    return (
        pl.BlockSpec((None, None, S, 2), lambda b, h: (b, h, 0, 0)),
        pl.BlockSpec((None, None, 2, S), lambda b, h: (b, h, 0, 0)),
    )


def mix_forward(act, sizes, accum, accum_turned, state_in, state_out, marks):
    T, wide = act.shape
    S = T // 2
    down, across = heads_specs(S)
    return pl.pallas_call(
        mix_kernel,
        grid=(2, wide // 128),
        in_specs=[by_columns(S), down, down, across]
        + [by_sequence(S)] * 2
        + marks_specs(S),
        out_specs=by_columns(S),
        out_shape=jax.ShapeDtypeStruct((T, wide), f32),
    )(act, sizes, accum, accum_turned, state_in, state_out, *marks)


def mix_backward(grad, act, sizes, accum, accum_turned, state_in, state_out, marks):
    T, wide = act.shape
    S = T // 2
    down, across = heads_specs(S)
    return pl.pallas_call(
        mix_back_kernel,
        grid=(2, wide // 128),
        in_specs=[by_columns(S), by_columns(S), down, down, across]
        + [by_sequence(S)] * 2
        + marks_specs(S),
        out_specs=[
            by_columns(S),
            down,
            pl.BlockSpec((None, S, S), lambda b, h: (b, 0, 0)),
            down,
            across,
        ],
        out_shape=[
            jax.ShapeDtypeStruct((T, wide), f32),
            jax.ShapeDtypeStruct(accum.shape, f32),
            jax.ShapeDtypeStruct((2, S, S), jnp.bfloat16),
            jax.ShapeDtypeStruct(accum.shape, f32),
            jax.ShapeDtypeStruct(accum_turned.shape, f32),
        ],
        scratch_shapes=[pltpu.VMEM((S, S), f32)],
    )(grad, act, sizes, accum, accum_turned, state_in, state_out, *marks)


def body(
    hidden,
    embedding,
    teacher_mid,
    teacher_out,
    segment_ids,
    rope_pos,
    valid_mask,
    gain_attn,
    w_query,
    w_key,
    w_value,
    query_down,
    query_up,
    w_attn_out,
    gain_mlp,
    w_gate,
    w_up,
    gate_down,
    gate_up,
    w_down,
    w_proj,
    gain_mamba,
    w_in_gate,
    w_in_main,
    w_in_state,
    w_in_step,
    conv_main,
    conv_main_bias,
    conv_state,
    conv_state_bias,
    gain_gated,
    w_mamba_out,
    step_bias,
    decay_log,
    skip_scale,
):
    me = Place()
    n_dp = me.n_dp
    S = hidden.shape[0]
    T = 2 * S
    quarter = S // 4
    z = me.z

    def own_rows(values):
        return lax.dynamic_slice_in_dim(values, me.tensor * quarter, quarter, 0)

    def own_tokens(values):
        return lax.dynamic_slice_in_dim(values, (z * 4 + me.tensor) * quarter, quarter, 0)

    def own_half(values, axis=-1):
        axis = axis % values.ndim
        width = values.shape[axis] // 2
        return lax.dynamic_slice_in_dim(values, z * width, width, axis)

    def filled(values, rows):
        fill = rows - values.shape[0]
        return jnp.pad(values, ((0, fill), (0, 128 - values.shape[1])))

    tiny = (
        gain_mlp,
        gain_mamba,
        conv_main,
        conv_main_bias,
        conv_state,
        conv_state_bias,
        gain_gated,
    )
    tiny_shapes = tuple(a.shape for a in tiny)
    tiny_pack = pack([a[None] for a in tiny], 1)[0]
    row_count = w_attn_out.shape[0]
    marks = jnp.stack([segment_ids, rope_pos])
    marks_other = me.hop(marks, "z")
    small = me.gather_packed(pack([gain_attn[None], query_up[None]], 1)[0])
    gain_attn_all, query_up_all = map(
        rows_joined, unpack(small, (gain_attn.shape, query_up.shape))
    )
    query_up_all = own_half(query_up_all)
    marks = jnp.stack([segment_ids, rope_pos])
    marks_other = me.hop(marks, "z")
    own_cat = jnp.concatenate([hidden, embedding], 1)
    gain_attn_f = gain_attn_all.astype(f32)
    normed_own = narrow(rms_scale(own_cat.astype(f32), gain_attn_f))
    normed_came = me.hop(own_rows(normed_own), "z")
    near_lane, far_lane = me.gates["pair"], me.gates["far"]
    swaps = {"query": me.swap(w_query)}
    near_lane += [small, marks_other]
    swaps["key"] = me.swap(w_key)
    near_lane += [normed_came]
    swaps["value"] = me.swap(w_value, extra=(query_down,))
    swaps["attn_out"] = me.swap(
        w_attn_out,
        extra=(
            gate_down,
            w_in_state,
            filled(gate_up.reshape(-1, 128), row_count),
            filled(w_in_step, row_count),
            filled(tiny_pack, row_count),
        ),
    )
    swaps["gate_up"] = me.swap(w_gate, w_up)
    swaps["late"] = me.swap(w_down, w_proj, w_in_gate, w_in_main, w_mamba_out)
    w_query_all = me.gather_weight(*swaps["query"])
    w_key_all = me.gather_weight(*swaps["key"])
    w_value_more = me.gather_weight(*swaps["value"])
    far_lane += [swaps["gate_up"][1]]
    attn_out_line = me.start_line("attn_out", *swaps["attn_out"])
    gate_up_line = me.start_line("gate_up", *swaps["gate_up"])
    w_attn_out_more = me.near_gather(me.finish_line("attn_out", attn_out_line))
    far_lane += [swaps["late"][1]]
    units = w_down.shape[1] // 2
    channels = w_in_gate.shape[1] // 2
    down_line, in_line = me.start_line(
        "late", *swaps["late"], [units + w_proj.shape[1] // 2, 3 * channels]
    )
    wide = w_value.shape[1] // 2
    w_value_all = w_value_more[:, :wide]
    query_down_all = w_value_more[:, wide:]

    def rows_back(columns, like):
        flat = columns.reshape(n_dp, -1, 128)[:, : like.size // 128]
        return rows_joined(me.restored(flat, 0).reshape((n_dp,) + like.shape))

    wide = w_attn_out.shape[1] // 2
    w_attn_out_all = w_attn_out_more[:, :wide]
    more = w_attn_out_more[:, wide:]
    gate_down_all = more[:, :128]
    w_in_state_all = more[:, 128:384]
    gate_up_all = own_half(rows_back(more[:, 384:512], gate_up))
    w_in_step_all = own_half(more[:, 512 : 512 + w_in_step.shape[1]])
    tiny_all = more[:, 640:].reshape(n_dp, -1, 128)[:, : tiny_pack.shape[0]]
    (
        gain_mlp_all,
        gain_mamba_all,
        conv_main_all,
        conv_main_bias_all,
        conv_state_all,
        conv_state_bias_all,
        gain_gated_all,
    ) = unpack(tiny_all, tiny_shapes)
    gain_mlp_all, gain_mamba_all = gain_mlp_all.reshape(-1), gain_mamba_all.reshape(-1)
    (
        conv_main_all,
        conv_main_bias_all,
        conv_state_all,
        conv_state_bias_all,
        gain_gated_all,
    ) = (
        rows_joined(me.restored(a, 0))
        for a in (
            conv_main_all,
            conv_main_bias_all,
            conv_state_all,
            conv_state_bias_all,
            gain_gated_all,
        )
    )
    conv_main_all = own_half(conv_main_all, 0).astype(f32)
    conv_main_bias_all = own_half(conv_main_bias_all, 0).astype(f32)
    gain_gated_f = own_half(gain_gated_all, 0).astype(f32)
    even = D // n_dp % 128 == 0
    order_d = me.columns_ordered(D) if even else [(0, D, 0)]
    hidden_shard, teacher_mid_shard, teacher_out_shard = move(
        [hidden, teacher_mid, teacher_out],
        [me.tensor * quarter],
        [(0, quarter)] * 3,
        [(i, c, w, i, None, to) for i in range(3) for c, w, to in order_d],
        [(quarter, D)] * 3,
    )
    if not even:
        hidden_shard = me.ordered(hidden_shard, 1)
        teacher_mid_shard = me.ordered(teacher_mid_shard, 1)
        teacher_out_shard = me.ordered(teacher_out_shard, 1)

    both = jnp.where(z == 0, jnp.stack([marks, marks_other], 1), jnp.stack([marks_other, marks], 1))
    segments, positions = both[0], both[1]
    marks_laid = (segments.reshape(T, 1), segments.reshape(2, 1, S))
    count = me.sum_everywhere(
        jnp.broadcast_to(jnp.sum(valid_mask.astype(f32)), (8, 128)), tensor=False
    )[0, 0]
    half = HEAD_SIZE // 2
    inverse = 10000.0 ** (-jnp.arange(half, dtype=f32) / half)
    angles = positions.reshape(T, 1).astype(f32) * inverse
    cosine = jnp.concatenate([jnp.cos(angles)] * 2, 1)
    sine = jnp.concatenate([-jnp.sin(angles), jnp.sin(angles)], 1)

    cat_shard = own_rows(own_cat).astype(f32)
    _, cat_back = jax.vjp(rms_scale, cat_shard, gain_attn_f)
    normed_other = me.gather_own(normed_came)
    normed_cat = place(
        [normed_own, normed_other], [z * S, (1 - z) * S], 0, T, me.columns_ordered(2 * D)
    )
    normed_cat_shard = own_tokens(normed_cat)
    normed_cat = me.after(normed_cat, "attn_out.far", "late.pair")
    query_low = narrow(times_right(normed_cat, query_down_all))
    query_pre = times_right(normed_cat, w_query_all) + times_right(query_low, query_up_all)
    key_pre = times_right(normed_cat, w_key_all)
    value_low = times_right(normed_cat, w_value_all, jnp.bfloat16)
    query_rot, key_rot, attended_low = attend_forward(
        query_pre, key_pre, value_low, cosine, sine, marks_laid
    )
    w_gate_up = me.near_gather(me.finish_line("gate_up", gate_up_line, hold=attended_low))
    w_down_proj = me.near_gather(me.finish_line("down", down_line))
    w_down_all = w_down_proj[:, :units]
    w_proj_all = w_down_proj[:, units:]
    attended_low = me.after(attended_low, "gate_up.line")
    attn_part = times_trans(attended_low, w_attn_out_all, jnp.bfloat16)
    attn_shard = me.reduce_tokens(attn_part)

    hidden_shard = hidden_shard.astype(f32)
    first_sum = hidden_shard + attn_shard
    normed_mid_f, mid_back = jax.vjp(rms_scale, first_sum, gain_mlp_all.astype(f32))
    normed_mid_shard = narrow(normed_mid_f)
    normed_mid = me.gather_tokens(me.after(normed_mid_shard, "down.line"))
    w_in_out = me.near_gather(me.finish_line("in", in_line, hold=normed_mid))
    w_in_all = w_in_out[:, : 2 * channels]
    w_mamba_out_all = w_in_out[:, 2 * channels :]
    gate_low = narrow(times_right(normed_mid, gate_down_all))
    gate_up_pre = times_right(normed_mid, w_gate_up)
    gate_pre = gate_up_pre[:, :units] + times_right(gate_low, gate_up_all)
    up_pre = gate_up_pre[:, units:]
    inner, inner_back = jax.vjp(gelu_product, gate_pre, up_pre)
    inner = narrow(inner)
    mlp_part = narrow(
        times_trans(w_down_all, inner) + times_trans(w_attn_out_all, attended_low)
    )
    mlp_part = me.after(mlp_part, "in.line")
    shared_out = narrow(me.reduce_features(mlp_part))
    projected = me.reduce_tokens(
        narrow(
            lax.dot_general(
                shared_out, w_proj_all, (((0,), (1,)), ((), ())), preferred_element_type=f32
            )
        )
    )
    middle = hidden_shard + projected

    normed_last_f, last_back = jax.vjp(rms_scale, middle, gain_mamba_all.astype(f32))
    normed_last_shard = narrow(normed_last_f)
    normed_last = me.gather_tokens(normed_last_shard)
    mamba_in = times_right(normed_last, w_in_all)
    mamba_gate = mamba_in[:, :channels].reshape(2, S, channels)
    mamba_pre = mamba_in[:, channels:].reshape(2, S, channels)
    state_pre = times_right(normed_last, w_in_state_all).reshape(2, S, 2 * STATE)
    mamba_here = w_in_step_all.shape[1]
    step_pre = times_right(normed_last, w_in_step_all).reshape(2, S, mamba_here)
    convolve = partial(conv_act, segments=segments)
    mamba_act, main_conv_back = jax.vjp(convolve, mamba_pre, conv_main_all, conv_main_bias_all)
    state_act, state_conv_back = jax.vjp(
        convolve, state_pre, conv_state_all.astype(f32), conv_state_bias_all.astype(f32)
    )
    state_in = narrow(state_act[..., :STATE])
    state_out = narrow(state_act[..., STATE:])
    (accum, step_sizes), decay_back = jax.vjp(
        decay_piece,
        step_pre,
        own_half(step_bias, 0).astype(f32),
        own_half(decay_log, 0).astype(f32),
    )
    sizes_down, _ = by_heads(step_sizes)
    accum_down, accum_across = by_heads(accum)
    act_flat = mamba_act.reshape(T, channels)
    in_flat, out_flat = state_in.reshape(T, STATE), state_out.reshape(T, STATE)
    mix_inputs = (act_flat, sizes_down, accum_down, accum_across, in_flat, out_flat, marks_laid)
    core = mix_forward(*mix_inputs).reshape(2, S, channels)
    mixed, mixed_back = jax.vjp(
        mixed_piece, core, mamba_act, mamba_gate, own_half(skip_scale, 0).astype(f32)
    )
    square_part = jnp.sum(mixed * mixed, axis=-1).reshape(2, 2, 2, 1, quarter)
    square_total = me.halve(square_part, "zxc", "cxz", f32).reshape(quarter)
    scaled = narrow(mixed * gain_gated_f).reshape(T, channels)
    mamba_sum = me.reduce_tokens(times_trans(scaled, w_mamba_out_all, jnp.bfloat16))
    inverse_rms = lax.rsqrt(square_total / DI + eps)[:, None]
    mamba_branch = inverse_rms * mamba_sum
    final_sum = middle + mamba_branch

    valid_rows = own_rows(valid_mask).astype(f32)[:, None]
    miss_mid = middle - teacher_mid_shard.astype(f32)
    miss_out = final_sum - teacher_out_shard.astype(f32)
    square_mid = jnp.sum(valid_rows * miss_mid * miss_mid)
    square_out = jnp.sum(valid_rows * miss_out * miss_out)
    factor = S * n_dp / count
    grad_final = factor * valid_rows * miss_out
    row_inner = jnp.sum(grad_final * mamba_branch, axis=-1)
    pull = row_inner * inverse_rms[:, 0] * inverse_rms[:, 0] / DI
    branch_grad = me.gather_tokens(narrow(inverse_rms * grad_final))
    pull_all = me.gather_small(pull).reshape(2, S, 1)

    dw_mamba_out = trans_times(branch_grad, scaled, jnp.bfloat16)
    sum_mamba_out = me.square_sum(dw_mamba_out)
    grad_scaled = times_right(branch_grad, w_mamba_out_all).reshape(2, S, channels)
    grad_gain_gated = jnp.sum(grad_scaled * mixed, axis=(0, 1))
    grad_mixed = grad_scaled * gain_gated_f - mixed * pull_all
    grad_core, grad_heads, grad_gate_z, grad_skip_scale = mixed_back(grad_mixed)
    act_part, dsize, gram_grad, dacc, dturned = mix_backward(
        narrow(grad_core).reshape(T, channels), *mix_inputs
    )

    def from_down(values):
        return values.transpose(0, 2, 1, 3).reshape(2, S, mamba_here)

    grad_accum = from_down(dacc) - dturned.reshape(2, mamba_here, S).transpose(0, 2, 1)
    grad_step_pre, grad_step_bias, grad_decay_log = decay_back((grad_accum, from_down(dsize)))
    grad_heads = grad_heads + act_part.reshape(2, S, channels)
    grad_state_part = jnp.concatenate(
        [
            jnp.einsum("bts,bte->bse", gram_grad, state_out, preferred_element_type=f32),
            jnp.einsum("bts,bse->bte", gram_grad, state_in, preferred_element_type=f32),
        ],
        axis=-1,
    )
    state_shard = me.reduce_tokens(narrow(grad_state_part).reshape(T, 2 * STATE))
    grad_state = me.gather_tokens(narrow(state_shard)).astype(f32).reshape(2, S, 2 * STATE)
    grad_mamba_pre, grad_conv_main, grad_conv_main_bias = main_conv_back(
        grad_heads.reshape(2, S, channels)
    )
    grad_in = jnp.concatenate([narrow(grad_gate_z), narrow(grad_mamba_pre)], -1).reshape(T, -1)
    step_grad_low = narrow(grad_step_pre).reshape(T, -1)
    sum_in = me.square_sum(trans_times(normed_last, grad_in, jnp.bfloat16))
    grad_w_in_step = me.restored(trans_times(normed_last, step_grad_low, jnp.bfloat16), 0)
    last_part = times_trans(grad_in, w_in_all) + times_trans(step_grad_low, w_in_step_all)
    last_part = lax.optimization_barrier((narrow(last_part), sum_mamba_out))[0]
    last_shard = me.reduce_tokens(last_part)
    grad_state_pre, grad_conv_state, grad_conv_state_bias = state_conv_back(grad_state)
    state_grad_low = own_tokens(narrow(grad_state_pre).reshape(T, -1))
    grad_w_in_state = trans_times(normed_last_shard, state_grad_low, jnp.bfloat16)
    grad_middle, grad_gain_mamba = last_back(
        last_shard + times_trans(state_grad_low, w_in_state_all)
    )
    grad_middle = grad_middle + grad_final + factor * valid_rows * miss_mid

    projected_grad = me.gather_tokens(narrow(grad_middle))
    sum_proj = me.near_sum(
        narrow(
            lax.dot_general(
                projected_grad, shared_out, (((0,), (1,)), ((), ())), preferred_element_type=f32
            )
        )
    )
    mlp_grad = me.gather_features(times_right(projected_grad, w_proj_all, jnp.bfloat16))
    mlp_grad = lax.optimization_barrier((mlp_grad, sum_in))[0]
    dw_down = trans_times(mlp_grad, inner, jnp.bfloat16)
    sum_down = me.near_sum(dw_down)
    grad_gate_pre, grad_up_pre = inner_back(times_right(mlp_grad, w_down_all))
    gate_grad = narrow(grad_gate_pre)
    up_grad = narrow(grad_up_pre)
    pre_grad = jnp.concatenate([gate_grad, up_grad], 1)
    dw_gate_up = trans_times(normed_mid, pre_grad, jnp.bfloat16)
    sum_gate_up = me.near_sum(dw_gate_up)
    mid_part = times_trans(pre_grad, w_gate_up, jnp.bfloat16)
    mid_part = lax.optimization_barrier((mid_part, dw_down, dw_gate_up))[0]
    low_part = times_trans(gate_grad, gate_up_all, jnp.bfloat16)
    mid_shard = me.reduce_tokens(mid_part)
    gate_low_grad = narrow(me.reduce_tokens(low_part))
    grad_w_gate, grad_w_up = me.scatter_unit("gate_up", sum_gate_up, parts=(2,))
    grad_gate_up = trans_times(gate_low, gate_grad, jnp.bfloat16)
    grad_gate_down = trans_times(normed_mid_shard, gate_low_grad, jnp.bfloat16)
    grad_first, grad_gain_mlp = mid_back(mid_shard + times_trans(gate_low_grad, gate_down_all))

    attn_grad_shard = narrow(own_tokens(mlp_grad).astype(f32) + grad_first)
    attn_grad = me.gather_tokens(attn_grad_shard)
    sum_attn_out = me.near_sum(trans_times(attn_grad, attended_low, jnp.bfloat16))
    attended_grad = times_right(attn_grad, w_attn_out_all, jnp.bfloat16)
    attended_grad = me.after(attended_grad, "gate_up.ready")
    query_grad, key_grad, value_grad = attend_backward(
        query_rot, key_rot, value_low, attended_grad, cosine, sine, marks_laid
    )
    sum_value = me.near_sum(trans_times(normed_cat, value_grad, jnp.bfloat16))
    sum_key = me.near_sum(trans_times(normed_cat, key_grad, jnp.bfloat16))
    sum_query = me.near_sum(trans_times(normed_cat, query_grad, jnp.bfloat16))
    cat_part = narrow(
        times_trans(query_grad, w_query_all)
        + times_trans(key_grad, w_key_all)
        + times_trans(value_grad, w_value_all)
    )
    low_part = times_trans(query_grad, query_up_all, jnp.bfloat16)
    cat_part = me.after(cat_part, "gate_up.sum")
    cat_shard_sum = me.reduce_tokens(cat_part)
    query_low_grad = narrow(me.reduce_tokens(low_part))
    def later(values):
        return lax.optimization_barrier((values, cat_shard_sum))[0]

    grad_w_proj, grad_w_down = me.scatter_unit("block", later(sum_proj), later(sum_down))
    grad_w_mamba_out, grad_w_in_gate, grad_w_in_main = me.join_halves(
        "mixer", later(sum_mamba_out), later(sum_in), parts=(1, 2)
    )
    (grad_w_attn_out,) = me.scatter_unit("d_attn_out", later(sum_attn_out))
    (grad_w_value,) = me.scatter_unit("d_value", later(sum_value))
    (grad_w_key,) = me.scatter_unit("key", sum_key)
    (grad_w_query,) = me.scatter_unit("query", sum_query)
    grad_query_up = trans_times(query_low, query_grad, jnp.bfloat16)
    grad_query_down = trans_times(normed_cat_shard, query_low_grad, jnp.bfloat16)
    grad_concat, grad_gain_attn = cat_back(
        me.restored_rows(cat_shard_sum + times_trans(query_low_grad, query_down_all))
    )
    stream = me.restored_rows(grad_first + grad_middle)
    grad_both = jnp.concatenate([grad_concat[:, :D] + stream, grad_concat[:, D:]], 1)
    grad_both = me.gather_own(narrow(grad_both)).astype(f32)
    if even:
        final_low = lax.optimization_barrier((narrow(final_sum), cat_part))[0]
        output = me.gather_own(final_low, me.columns_restored(D))
    else:
        output = me.gather_own(me.restored(narrow(final_sum), 1))

    def by_dp(values):
        return values.reshape((n_dp, values.shape[0] // n_dp) + values.shape[1:])

    def both_halves(values, axis):
        axis = axis % values.ndim
        nothing = jnp.zeros_like(values)
        return jnp.where(
            z == 0,
            jnp.concatenate([values, nothing], axis),
            jnp.concatenate([nothing, values], axis),
        )

    first = (me.tensor == 0) & (z == 0)
    shared = (
        me.restored(grad_gain_mlp, 0),
        me.restored(grad_gain_mamba, 0),
        jnp.where(first, grad_conv_state, 0.0),
        jnp.where(first, grad_conv_state_bias, 0.0),
        me.restored(grad_gate_down, 0),
        me.restored(grad_w_in_state, 0),
    )
    shared_out_shapes = (
        gain_mlp.shape,
        gain_mamba.shape,
        conv_state.shape,
        conv_state_bias.shape,
        gate_down.shape,
        w_in_state.shape,
    )
    shared += (grad_gain_attn, me.restored(grad_query_down, 0))
    shared_out_shapes += (gain_attn.shape, query_down.shape)
    split = (
        both_halves(grad_conv_main, 0),
        both_halves(grad_conv_main_bias, 0),
        both_halves(grad_gain_gated, 0),
        both_halves(grad_gate_up, 1),
        both_halves(grad_w_in_step, 1),
        both_halves(grad_query_up, 1),
    )
    split_shapes = (
        conv_main.shape,
        conv_main_bias.shape,
        gain_gated.shape,
        gate_up.shape,
        w_in_step.shape,
        query_up.shape,
    )
    shared_rows = pack([by_dp(narrow(a)) for a in shared], n_dp)
    part_rows = shared_rows.shape[1] // 4
    blocks = shared_rows.reshape(n_dp, 2, 2, part_rows, 128).transpose(1, 2, 0, 3, 4)
    shared_mine = narrow(me.halve(blocks, "xc", "cx"))
    split_rows = pack([by_dp(narrow(a)) for a in split], n_dp)
    small_mine = me.sum_dp(rows_joined(jnp.concatenate([shared_mine, split_rows], 1)))
    shared_sum = me.gather_own(small_mine[:part_rows])
    (
        out_gain_mlp,
        out_gain_mamba,
        out_conv_state,
        out_conv_state_bias,
        out_gate_down,
        out_w_in_state,
        out_gain_attn,
        out_query_down,
    ) = [v[0].astype(f32) for v in unpack(shared_sum[None], shared_out_shapes)]
    (
        out_conv_main,
        out_conv_main_bias,
        out_gain_gated,
        out_gate_up,
        out_w_in_step,
        out_query_up,
    ) = [v[0].astype(f32) for v in unpack(small_mine[None, part_rows:], split_shapes)]
    grad_step_bias, grad_decay_log, grad_skip_scale, square_mid, square_out = (
        lax.optimization_barrier(
            (grad_step_bias, grad_decay_log, grad_skip_scale, square_mid, square_out, cat_part)
        )[:5]
    )
    head_rows = jnp.stack(
        [
            both_halves(grad_step_bias, 0),
            both_halves(grad_decay_log, 0),
            both_halves(grad_skip_scale, 0),
        ]
    )
    head_sums = me.sum_everywhere(head_rows, tensor=False)
    losses = me.sum_everywhere(
        jnp.stack(
            [jnp.broadcast_to(square_mid, (128,)), jnp.broadcast_to(square_out, (128,))]
        )
    )
    loss_mid = losses[0, 0] / (count * D)
    loss_out = losses[1, 0] / (count * D)
    return (
        output,
        loss_mid,
        loss_out,
        grad_both[:, :D],
        grad_both[:, D:],
        out_gain_attn,
        grad_w_query,
        grad_w_key,
        grad_w_value,
        out_query_down,
        out_query_up,
        grad_w_attn_out,
        out_gain_mlp,
        grad_w_gate,
        grad_w_up,
        out_gate_down,
        out_gate_up,
        grad_w_down,
        grad_w_proj,
        out_gain_mamba,
        grad_w_in_gate,
        grad_w_in_main,
        out_w_in_state,
        out_w_in_step,
        out_conv_main,
        out_conv_main_bias,
        out_conv_state,
        out_conv_state_bias,
        out_gain_gated,
        grad_w_mamba_out,
        head_sums[0],
        head_sums[1],
        head_sums[2],
    )


def solution(mesh):
    in_specs = (
        P("dp", None),
        P("dp", None),
        P("dp", None),
        P("dp", None),
        P("dp"),
        P("dp"),
        P("dp"),
        P("dp"),
        P("dp", "tensor"),
        P("dp", "tensor"),
        P("dp", "tensor"),
        P("dp", None),
        P("dp", "tensor"),
        P("dp", "tensor"),
        P("dp"),
        P("dp", "tensor"),
        P("dp", "tensor"),
        P("dp", None),
        P("dp", "tensor"),
        P("dp", "tensor"),
        P("dp", "tensor"),
        P("dp"),
        P("dp", "tensor"),
        P("dp", "tensor"),
        P("dp", None),
        P("dp", "tensor"),
        P(("tensor", "dp"), None),
        P(("tensor", "dp")),
        P("dp", None),
        P("dp"),
        P(("tensor", "dp")),
        P("dp", "tensor"),
        P("tensor"),
        P("tensor"),
        P("tensor"),
    )
    out_specs = (
        P("dp", None),
        P(),
        P(),
        P("dp", None),
        P("dp", None),
        P("dp"),
        P("dp", "tensor"),
        P("dp", "tensor"),
        P("dp", "tensor"),
        P("dp", None),
        P("dp", "tensor"),
        P("dp", "tensor"),
        P("dp"),
        P("dp", "tensor"),
        P("dp", "tensor"),
        P("dp", None),
        P("dp", "tensor"),
        P("dp", "tensor"),
        P("dp", "tensor"),
        P("dp"),
        P("dp", "tensor"),
        P("dp", "tensor"),
        P("dp", None),
        P("dp", "tensor"),
        P(("tensor", "dp"), None),
        P(("tensor", "dp")),
        P("dp", None),
        P("dp"),
        P(("tensor", "dp")),
        P("dp", "tensor"),
        P("tensor"),
        P("tensor"),
        P("tensor"),
    )
    return jax.shard_map(body, mesh=mesh, in_specs=in_specs, out_specs=out_specs, check_vma=False)
```
